128 devices in a mesh: req: 16 (over y, z_hi, core), tp: 8 (over x, z_lo).
Axes of the slice: x: 4, y: 4, z: 4 (z_hi: 2, z_lo: 2; z = z_hi * 2 + z_lo), core: 2. Of those that a mesh axis runs over, the one named last changes fastest.
Arguments:
- hidden: bfloat16 [64, 128, 7168], P('req', None, 'tp'), may hold values from -7 to 7
- norm_gain: float32 [7168], replicated, may hold values from 0.5 to 1.5
- w_query: bfloat16 [7168, 4096], P(None, 'tp'), may hold values from -13 to 13
- w_kv: bfloat16 [7168, 2, 1024], P(None, None, 'tp'), may hold values from -13 to 13
- w_out: bfloat16 [4096, 7168], P('tp'), may hold values from -0.09375 to 0.09375
- prefix_cache: bfloat16 [16, 2048, 2, 1024], P('req', None, None, 'tp'), may hold values from -60 to 60
- lengths: int32 [64], P('req'), may hold values from 1 to 128, as said below
- groups: int32 [64], replicated, may hold values from 0 to 15, as said below
- owners: int32 [16], replicated, may hold values from 0 to 15, each once
Outputs:
- out_hidden: bfloat16 [64, 128, 7168], P('req', None, 'tp')
- suffix_cache: bfloat16 [64, 128, 2, 1024], P('req', None, None, 'tp')
The draws below stay inside these ranges and needn't reach their ends.
Inputs may be any that keep to these rules, and one draw needn't show every extreme that they name: `lengths`: some request has all 128 positions live in every draw. The 4 requests of one req index belong to different groups; exactly one group has 8 requests; every other group has at most 4. `owners`: each req index once.
All inputs are finite; a program needn't handle non-finite values.
Results may differ from the reference program's by a relative error of at most 0.014.
Values may be sent and summed in bfloat16 or wider, within the bound.
A program may use at most 192 MiB of HBM per device.

```python
import jax
import jax.numpy as jnp
from jax import lax

D = 7168
HD = 128
GROUP = 4
SUF = 128
PREFIX = 2048
REQ_DEV = 4
KVH = 8
HEADS = 32
REQUESTS = 64
N_REQ = 16


def draw_prefix_cache(key, part):
    shape = (N_REQ, PREFIX, 2, KVH * HD)
    values = jnp.clip(jax.random.normal(key, shape, jnp.float32), -6.0, 6.0)
    return values.astype(jnp.bfloat16)


def draw_hidden(key, part):
    noise = jnp.clip(jax.random.normal(jax.random.fold_in(key, 21), (REQUESTS, SUF, D), jnp.float32), -6.0, 6.0)
    return noise.astype(jnp.bfloat16)


def key_weights(key):
    base = jax.random.normal(jax.random.fold_in(key, 102), (D, KVH, HD), jnp.float32)
    return jnp.clip(base, -6.0, 6.0) * D ** (-0.5)


def draw_w_kv(key, part):
    keys_part = key_weights(key)
    values_part = jnp.clip(jax.random.normal(jax.random.fold_in(key, 104), (D, KVH, HD), jnp.float32), -6.0, 6.0) * D ** (-0.5)
    stacked = jnp.stack([keys_part, values_part], axis=1)
    return stacked.reshape(D, 2, KVH * HD).astype(jnp.bfloat16)


def draw_w_query(key, part):
    own = jnp.clip(jax.random.normal(jax.random.fold_in(key, 103), (D, KVH, GROUP, HD), jnp.float32), -6.0, 6.0) * D ** (-0.5)
    return own.reshape(D, KVH * GROUP * HD).astype(jnp.bfloat16)


def draw_lengths(key, part):
    drawn = jax.random.randint(jax.random.fold_in(key, 1), (REQUESTS,), 1, SUF + 1)
    longest = jax.random.randint(jax.random.fold_in(key, 2), (), 0, REQUESTS)
    return jnp.where(jnp.arange(REQUESTS) == longest, SUF, drawn).astype(jnp.int32)


def draw_groups(key, part):
    busiest = jax.random.randint(jax.random.fold_in(key, 1), (), 0, N_REQ)
    device_ids = jnp.arange(N_REQ)[:, None]
    slot_ids = jnp.arange(REQ_DEV)[None, :]
    base = (device_ids + slot_ids) % N_REQ
    offset = (busiest - device_ids) % N_REQ
    donor = (offset >= REQ_DEV) & (offset < 2 * REQ_DEV)
    labels = jnp.where(donor & (slot_ids == 0), busiest, base)
    relabel = jax.random.permutation(jax.random.fold_in(key, 2), N_REQ).astype(jnp.int32)
    labels = jnp.take(relabel, labels, axis=0)
    device_order = jax.random.permutation(jax.random.fold_in(key, 3), N_REQ).astype(jnp.int32)
    labels = jnp.take(labels, device_order, axis=0)
    return labels.reshape(REQUESTS).astype(jnp.int32)


def steps_of(stream_key, dims, shards, low, largest):
    loudness = 1.0
    for dim, parts in shards:
        draws = jax.random.uniform(jax.random.fold_in(jax.random.fold_in(stream_key, 6), dim), (parts,), jnp.float32, low / len(shards), largest / len(shards))
        loudness = loudness * jnp.repeat(jnp.exp(draws), dims[dim] // parts).reshape((-1,) + (1,) * (len(dims) - 1 - dim))
    return loudness


def scatter_about(stream_key, extent, spread, limit, split=(), kind=jnp.bfloat16):
    entries = jax.random.normal(stream_key, extent, jnp.float32) * spread
    if len(split) > 0:
        entries = steps_of(stream_key, extent, split, -0.22, 0.18) * entries
    return jnp.clip(entries, min=-limit, max=limit).astype(kind)


def setup_inputs(seed: int = 0) -> dict:
    arg_keys = jax.random.split(jax.random.key(seed), 10)
    hidden = draw_hidden(jax.random.fold_in(arg_keys[9], 71), 0)
    norm_gain = jnp.clip(1.0 + 0.1 * jax.random.normal(arg_keys[1], (D,), jnp.float32), 0.5, 1.5)
    w_query = draw_w_query(jax.random.fold_in(arg_keys[9], 71), 0)
    w_kv = draw_w_kv(jax.random.fold_in(arg_keys[9], 71), 0)
    w_out = scatter_about(arg_keys[4], (HEADS * HD, D), (HEADS * HD) ** -0.5, 0.09375, ((0, 8),))
    prefix_cache = draw_prefix_cache(jax.random.fold_in(arg_keys[9], 71), 0)
    lengths = draw_lengths(jax.random.fold_in(arg_keys[9], 71), 0)
    groups = draw_groups(jax.random.fold_in(arg_keys[9], 71), 0)
    owners = jax.random.permutation(arg_keys[8], N_REQ).astype(jnp.int32)
    return {"hidden": hidden, "norm_gain": norm_gain, "w_query": w_query, "w_kv": w_kv, "w_out": w_out, "prefix_cache": prefix_cache, "lengths": lengths, "groups": groups, "owners": owners}


EPSILON = 1e-05
ROPE_BASE = 5000000.0

def rope_tables():
    positions = (PREFIX + jnp.arange(SUF)).astype(jnp.float32)
    inverse = ROPE_BASE ** (-(2.0 * jnp.arange(HD // 2).astype(jnp.float32)) / HD)
    angles = positions[:, None] * inverse[None, :]
    cosine_table = jnp.concatenate([jnp.cos(angles), jnp.cos(angles)], axis=-1)
    sine_table = jnp.concatenate([jnp.sin(angles), jnp.sin(angles)], axis=-1)
    return (cosine_table, sine_table)

def rotate(vector, cosine_table, sine_table):
    half_size = vector.shape[-1] // 2
    turned = jnp.concatenate([-vector[..., half_size:], vector[..., :half_size]], axis=-1)
    return vector * cosine_table + turned * sine_table

def soft_part(scores, values_f, form):
    highest = lax.optimization_barrier(jnp.max(scores, axis=-1))
    weights = jnp.exp(scores - highest[..., None])
    totals = lax.optimization_barrier(jnp.sum(weights, axis=-1))
    rounded = lax.optimization_barrier(weights.astype(jnp.bfloat16)).astype(jnp.float32)
    output = jnp.einsum(form, rounded, values_f) / totals[..., None]
    return (output, highest + jnp.log(totals))

def reference(hidden, norm_gain, w_query, w_kv, w_out, prefix_cache, lengths, groups, owners):
    residual = hidden.astype(jnp.float32)
    normed = (residual * lax.rsqrt(lax.optimization_barrier(jnp.mean(residual * residual, axis=-1, keepdims=True)) + EPSILON) * norm_gain).astype(jnp.bfloat16)
    normed_rows = normed.reshape(REQUESTS * SUF, D)
    queries = jnp.dot(normed_rows, w_query, preferred_element_type=jnp.float32).reshape(REQUESTS, SUF, KVH, GROUP, HD)
    key_value = jnp.dot(normed_rows, w_kv.reshape(D, 2 * KVH * HD), preferred_element_type=jnp.float32).reshape(REQUESTS, SUF, 2, KVH, HD)
    cosine_table, sine_table = rope_tables()
    queries = rotate(queries, cosine_table[None, :, None, None, :], sine_table[None, :, None, None, :]).astype(jnp.bfloat16)
    rotated = rotate(key_value[:, :, 0], cosine_table[None, :, None, :], sine_table[None, :, None, :])
    kv_rows = jnp.stack([rotated, key_value[:, :, 1]], axis=2).astype(jnp.bfloat16)
    position_ids = jnp.arange(SUF)
    live_rows = position_ids[None, :] < lengths[:, None]
    suffix_cache = jnp.where(live_rows[:, :, None, None, None], kv_rows, jnp.zeros_like(kv_rows)).reshape(REQUESTS, SUF, 2, KVH * HD)
    slot_ids = lax.optimization_barrier(jnp.sum(jnp.where(groups[:, None] == jnp.arange(N_REQ)[None, :], owners[None, :], 0), axis=-1)).astype(jnp.int32)
    score_scale = HD ** (-0.5)

    def attend(request):
        one_query, one_kv, length, slot = request
        query_f = one_query.astype(jnp.float32)
        block_kv = lax.dynamic_index_in_dim(prefix_cache, slot, 0, keepdims=False).reshape(PREFIX, 2, KVH, HD).astype(jnp.float32)
        prefix_scores = jnp.einsum('tkgd,pkd->tkgp', query_f, block_kv[:, 0]) * score_scale
        prefix_out, prefix_lse = soft_part(prefix_scores, block_kv[:, 1], 'tkgp,pkd->tkgd')
        own_kv = one_kv.astype(jnp.float32)
        suffix_scores = jnp.einsum('tkgd,skd->tkgs', query_f, own_kv[:, 0]) * score_scale
        causal = (position_ids[None, :] <= position_ids[:, None]) & (position_ids[None, :] < length)
        suffix_scores = jnp.where(causal[:, None, None, :], suffix_scores, -jnp.inf)
        suffix_out, suffix_lse = soft_part(suffix_scores, own_kv[:, 1], 'tkgs,skd->tkgd')
        highest = jnp.maximum(prefix_lse, suffix_lse)
        prefix_share = jnp.exp(prefix_lse - highest)
        suffix_share = jnp.exp(suffix_lse - highest)
        mixed_out = (prefix_share[..., None] * prefix_out + suffix_share[..., None] * suffix_out) / (prefix_share + suffix_share)[..., None]
        return mixed_out.astype(jnp.bfloat16)
    attention = lax.map(attend, (queries, kv_rows, lengths, slot_ids))
    attention_rows = attention.reshape(REQUESTS * SUF, KVH, GROUP * HD)
    out_blocks = w_out.reshape(KVH, GROUP * HD, D)
    summed = jnp.zeros((REQUESTS * SUF, D), jnp.float32)
    for kv_head in range(KVH):
        partial_value = jnp.dot(attention_rows[:, kv_head], out_blocks[kv_head], preferred_element_type=jnp.float32).astype(jnp.bfloat16)
        summed = summed + lax.optimization_barrier(partial_value).astype(jnp.float32)
    mixed = residual + summed.reshape(REQUESTS, SUF, D)
    out_hidden = jnp.where(live_rows[:, :, None], mixed, 0.0).astype(jnp.bfloat16)
    return (out_hidden, suffix_cache)
```

```python
import functools

import jax
import jax.numpy as jnp
from jax import lax
from jax.experimental import pallas as pl
from jax.experimental.pallas import tpu as pltpu
from jax.sharding import PartitionSpec as P

PREFIX = 2048
EPSILON = 1e-05
ROPE_BASE = 5000000.0
MESH = pl.DeviceIdType.MESH
BF = jnp.bfloat16
F32 = jnp.float32

ROWS = 512
FEAT = 896
HD = 128

GB = 48
G_H1, G_H2 = (0, 256), (256, 256)
G_A1, G_A2 = (GB, 256 - GB), (256, 256 - GB)
G_B1, G_B2 = (0, GB), (512 - GB, GB)
SB = 112
SA = 256 - SB


def rope_tables(suffix_len, head_size):
    positions = (PREFIX + jnp.arange(suffix_len)).astype(F32)
    inverse = ROPE_BASE ** (-(2.0 * jnp.arange(head_size // 2).astype(F32)) / head_size)
    angles = positions[:, None] * inverse[None, :]
    cosine = jnp.concatenate([jnp.cos(angles), jnp.cos(angles)], axis=-1)
    sine = jnp.concatenate([-jnp.sin(angles), jnp.sin(angles)], axis=-1)
    return cosine, sine


def places():
    req, tp = lax.axis_index("req"), lax.axis_index("tp")
    x, zl = tp // 2, tp % 2
    y, low = req // 4, req % 4
    zh, core = low // 2, low % 2
    other_z = 1 - zl

    def at(xx, zz):
        return {"req": req, "tp": xx * 2 + zz}

    def own(yy, hh, cc):
        return {"req": yy * 4 + hh * 2 + cc, "tp": tp}

    return dict(
        req=req, tp=tp, x=x, zl=zl, y=y, zh=zh, core=core, oz=other_z,
        xp=at((x + 1) % 4, zl), xm=at((x + 3) % 4, zl), zp=at(x, other_z),
        yp=own((y + 1) % 4, zh, core), ym=own((y + 3) % 4, zh, core),
        zz=own(y, 1 - zh, core), cc=own(y, zh, 1 - core),
    )


def barrier(devices):
    sem = pltpu.get_barrier_semaphore()
    for d in devices:
        pl.semaphore_signal(sem, inc=1, device_id=d, device_id_type=MESH)
    pl.semaphore_wait(sem, len(devices))


class Mail:
    def __init__(self, send_sems, recv_sems):
        self.send_sems, self.recv_sems, self.made = send_sems, recv_sems, {}

    def send(self, name, src, dst, device):
        i = len(self.made)
        c = pltpu.make_async_remote_copy(
            src_ref=src, dst_ref=dst, send_sem=self.send_sems.at[i], recv_sem=self.recv_sems.at[i],
            device_id=device, device_id_type=MESH)
        c.start()
        self.made[name] = c

    def recv(self, *names):
        for name in names:
            self.made[name].wait_recv()

    def drain(self):
        for c in self.made.values():
            c.wait_send()


N_GATHER = 52


def gather_kernel(hid, pre, wq, wkv, gain, cos, sin, q_o, k_o, v_o, pout,
                  xbuf, wq_v, wkv_v, wf, wkvd, praw, pst, acc, sq, send_sems, recv_sems, loc):
    p = places()
    tp, x, zl, oz = p["tp"], p["x"], p["zl"], p["oz"]
    barrier([p[k] for k in ("xp", "xm", "zp", "yp", "ym", "zz", "cc")])
    m = Mail(send_sems, recv_sems)

    def local(src, dst, i):
        c = pltpu.make_async_copy(src, dst, loc.at[i])
        c.start()
        return c

    def rows(ref, part):
        return ref.at[pl.ds(part[0], part[1])]

    def shard(xx, zz, part):
        return rows(xbuf.at[xx * 2 + zz], part)

    cp_pre = local(pre, praw, 0)
    own = lambda part: rows(hid, part)
    m.send("zA1", own(G_A1), shard(x, zl, G_A1), p["zp"])
    m.send("xp1", own(G_H1), shard(x, zl, G_H1), p["xp"])
    m.send("xm2", own(G_H2), shard(x, zl, G_H2), p["xm"])
    m.send("zA2", own(G_A2), shard(x, zl, G_A2), p["zp"])
    m.send("xp2", own(G_H2), shard(x, zl, G_H2), p["xp"])
    m.send("xm1", own(G_H1), shard(x, zl, G_H1), p["xm"])
    cp_x = local(hid, xbuf.at[tp], 1)
    cp_wq = local(wq, wq_v, 2)
    cp_wkv = local(wkv, wkv_v, 3)

    cp_pre.wait()

    @pl.loop(0, 4)
    def _(i):
        wf[pl.ds(0, 1024), :] = praw[pl.ds(pl.multiple_of(i * 1024, 1024), 1024), :].astype(F32)
        at = pl.ds(pl.multiple_of(i * 512, 512), 512)
        pst[0, at, :] = wf[pl.ds(0, 512, stride=2), :].astype(BF)
        pst[1, at, :] = wf[pl.ds(1, 512, stride=2), :].astype(BF)

    req, y, zh, core = p["req"], p["y"], p["zh"], p["core"]

    def pidx(yy, hh):
        return (yy % 4) * 4 + hh * 2 + core

    def to_core(name, yy, hh, kv):
        r = pout.at[pidx(yy, hh), kv]
        m.send("c" + name, r, r, p["cc"])

    def pass_on(name, yy, hh, kv, key):
        r = pout.at[pidx(yy, hh), kv]
        m.send(name, r, r, p[key])

    me = pidx(y, zh)
    for name, kv, key in (("zzK", 0, "zz"), ("ypK", 0, "yp"), ("ymV", 1, "ym"),
                          ("zzV", 1, "zz"), ("ypV", 1, "yp"), ("ymK", 0, "ym")):
        m.send(name, pst.at[kv], pout.at[me, kv], p[key])
    m.send("c0K", pst.at[0], pout.at[me, 0], p["cc"])
    m.send("c0V", pst.at[1], pout.at[me, 1], p["cc"])
    cp_p = local(pst, pout.at[me], 4)
    m.send("b01", own(G_B1), shard(x, zl, G_B1), p["zp"])
    m.send("b02", own(G_B2), shard(x, zl, G_B2), p["zp"])

    acc[...] = jnp.zeros_like(acc)
    sq[...] = jnp.zeros_like(sq)

    def compute(first, count, step, zz):
        @pl.loop(0, count)
        def _(j):
            s = ((first + step * j) % 4) * 2 + zz
            at = pl.multiple_of(s * FEAT, FEAT)
            wf[...] = wkv_v[pl.ds(pl.multiple_of(s * 2 * FEAT, 2 * FEAT), 2 * FEAT), :].astype(F32)
            wkvd[:, 0:HD] = wf[pl.ds(0, FEAT, stride=2), :].astype(BF)
            wkvd[:, HD:2 * HD] = wf[pl.ds(1, FEAT, stride=2), :].astype(BF)
            g = gain[s]

            @pl.loop(0, 2)
            def _(h):
                rr = pl.ds(pl.multiple_of(h * 256, 256), 256)
                xv = xbuf[s, rr, :].astype(F32)
                x2 = xv * xv
                t = x2[:, 0:128]
                for b in range(1, FEAT // 128):
                    t += x2[:, b * 128:(b + 1) * 128]
                sq[rr, :] += t
                xg = (xv * g).astype(BF)
                acc[rr, 0:512] += jnp.dot(xg, wq_v[pl.ds(at, FEAT), :], preferred_element_type=F32)
                acc[rr, 512:768] += jnp.dot(xg, wkvd[...], preferred_element_type=F32)

    cp_x.wait()
    cp_wq.wait()
    cp_wkv.wait()
    compute(x, 1, 1, zl)

    xb, xf, xo = (x + 3) % 4, (x + 1) % 4, (x + 2) % 4
    m.recv("xp1")
    m.send("fx1", shard(xb, zl, G_H1), shard(xb, zl, G_H1), p["xp"])
    m.recv("xm2")
    m.send("fx2", shard(xf, zl, G_H2), shard(xf, zl, G_H2), p["xm"])
    m.send("b11", shard(xb, zl, G_B1), shard(xb, zl, G_B1), p["zp"])
    m.send("b22", shard(xf, zl, G_B2), shard(xf, zl, G_B2), p["zp"])
    m.recv("ypK")
    cp_p.wait()
    pass_on("fyK", y + 3, zh, 0, "yp")
    to_core("1K", y + 3, zh, 0)
    m.recv("ymV")
    pass_on("fyV", y + 1, zh, 1, "ym")
    to_core("2V", y + 1, zh, 1)
    m.recv("zA1", "zA2")
    m.send("pxp1", shard(x, oz, G_A1), shard(x, oz, G_A1), p["xp"])
    m.send("pxm2", shard(x, oz, G_A2), shard(x, oz, G_A2), p["xm"])
    m.send("pxp2", shard(x, oz, G_A2), shard(x, oz, G_A2), p["xp"])
    m.send("pxm1", shard(x, oz, G_A1), shard(x, oz, G_A1), p["xm"])
    m.recv("xp2", "xm1")
    m.send("b12", shard(xb, zl, G_B2), shard(xb, zl, G_B2), p["zp"])
    m.send("b21", shard(xf, zl, G_B1), shard(xf, zl, G_B1), p["zp"])
    m.recv("ypV", "ymK")
    to_core("1V", y + 3, zh, 1)
    to_core("2K", y + 1, zh, 0)
    compute(x + 3, 2, 2, zl)
    m.recv("zzK")
    oh = 1 - zh
    pass_on("zypK", y, oh, 0, "yp")
    pass_on("zymK", y, oh, 0, "ym")
    to_core("3K", y, oh, 0)
    m.recv("fx1", "fx2")
    m.send("b31", shard(xo, zl, G_B1), shard(xo, zl, G_B1), p["zp"])
    m.send("b32", shard(xo, zl, G_B2), shard(xo, zl, G_B2), p["zp"])
    m.recv("fyK", "fyV")
    to_core("4K", y + 2, zh, 0)
    to_core("4V", y + 2, zh, 1)
    compute(x + 2, 1, 1, zl)
    m.recv("zzV")
    pass_on("zymV", y, oh, 1, "ym")
    pass_on("zypV", y, oh, 1, "yp")
    to_core("3V", y, oh, 1)
    m.recv("b01", "b02")
    compute(x, 1, 1, oz)
    m.recv("pxp1")
    m.send("fpx1", shard(xb, oz, G_A1), shard(xb, oz, G_A1), p["xp"])
    m.recv("pxm2")
    m.send("fpx2", shard(xf, oz, G_A2), shard(xf, oz, G_A2), p["xm"])
    m.recv("zypK")
    pass_on("fzK", y + 3, oh, 0, "yp")
    to_core("5K", y + 3, oh, 0)
    m.recv("pxp2", "pxm1", "b11", "b22", "b12", "b21")
    compute(x + 3, 2, 2, oz)
    m.recv("zymV")
    pass_on("fzV", y + 1, oh, 1, "ym")
    to_core("6V", y + 1, oh, 1)
    m.recv("fpx1", "fpx2", "b31", "b32")
    compute(x + 2, 1, 1, oz)

    c, s = cos[...], sin[...]

    @pl.loop(0, 4)
    def _(r):
        rr = pl.ds(pl.multiple_of(r * 128, 128), 128)
        mean = jnp.sum(sq[rr, :], axis=-1, keepdims=True) * (1.0 / (8 * FEAT))
        scale = lax.rsqrt(mean + EPSILON)
        for g in range(4):
            v = acc[rr, g * HD:(g + 1) * HD] * scale
            q_o[rr, g * HD:(g + 1) * HD] = (v * c + pltpu.roll(v, HD // 2, 1) * s).astype(BF)
        v = acc[rr, 512:640] * scale
        k_o[rr, :] = (v * c + pltpu.roll(v, HD // 2, 1) * s).astype(BF)
        v_o[rr, :] = (acc[rr, 640:768] * scale).astype(BF)

    m.recv("zypV")
    to_core("5V", y + 3, oh, 1)
    m.recv("zymK")
    to_core("6K", y + 1, oh, 0)
    m.recv("fzK")
    to_core("7K", y + 2, oh, 0)
    m.recv("fzV")
    to_core("7V", y + 2, oh, 1)
    for i in range(8):
        m.recv("c%dK" % i, "c%dV" % i)
    m.drain()
    assert len(m.made) == N_GATHER, len(m.made)


def gather_call(hid, pre, wq, wkv, gain, cos, sin):
    vm, hbm = pl.BlockSpec(memory_space=pltpu.VMEM), pl.BlockSpec(memory_space=pl.ANY)
    return pl.pallas_call(
        gather_kernel,
        out_shape=(
            jax.ShapeDtypeStruct((ROWS, 512), BF),
            jax.ShapeDtypeStruct((ROWS, HD), BF),
            jax.ShapeDtypeStruct((ROWS, HD), BF),
            jax.ShapeDtypeStruct((16, 2, PREFIX, HD), BF),
        ),
        in_specs=[hbm, hbm, hbm, hbm, vm, vm, vm],
        out_specs=(vm, vm, vm, hbm),
        scratch_shapes=[
            pltpu.VMEM((8, ROWS, FEAT), BF),
            pltpu.VMEM((8 * FEAT, 512), BF),
            pltpu.VMEM((16 * FEAT, HD), BF),
            pltpu.VMEM((2 * FEAT, HD), F32),
            pltpu.VMEM((FEAT, 2 * HD), BF),
            pltpu.VMEM((2 * PREFIX, HD), BF),
            pltpu.VMEM((2, PREFIX, HD), BF),
            pltpu.VMEM((ROWS, 768), F32),
            pltpu.VMEM((ROWS, HD), F32),
            pltpu.SemaphoreType.DMA((N_GATHER,)),
            pltpu.SemaphoreType.DMA((N_GATHER,)),
            pltpu.SemaphoreType.DMA((5,)),
        ],
        compiler_params=pltpu.CompilerParams(
            collective_id=0, has_side_effects=True, vmem_limit_bytes=56 << 20),
        name="gather",
    )(hid, pre, wq, wkv, gain, cos, sin)


def attention_kernel(own_ref, len_ref, q_ref, k_ref, v_ref, p_ref, o_ref, q4, o4):
    r = pl.program_id(0)
    length = len_ref[r]
    factor = (HD ** -0.5) * 1.4426950408889634
    for g in range(4):
        q4[g * 128:(g + 1) * 128, :] = q_ref[:, g * HD:(g + 1) * HD]
    contract = (((1,), (1,)), ((), ()))

    @pl.loop(0, 2)
    def _(i):
        rr = pl.ds(pl.multiple_of(i * 256, 256), 256)
        q = q4[rr, :]
        s1 = lax.dot_general(q, p_ref[0, 0], contract, preferred_element_type=F32)
        s2 = lax.dot_general(q, k_ref[...], contract, preferred_element_type=F32)
        t = lax.broadcasted_iota(jnp.int32, (256, 128), 0) % 128
        s = lax.broadcasted_iota(jnp.int32, (256, 128), 1)
        s2 = jnp.where((s <= t) & (s < length), s2, -jnp.inf)
        top = jnp.maximum(jnp.max(s1, axis=-1, keepdims=True), jnp.max(s2, axis=-1, keepdims=True))
        w1 = jnp.exp2((s1 - top) * factor)
        w2 = jnp.exp2((s2 - top) * factor)
        total = jnp.sum(w1, axis=-1, keepdims=True) + jnp.sum(w2, axis=-1, keepdims=True)
        out = jnp.dot(w1.astype(BF), p_ref[0, 1], preferred_element_type=F32)
        out += jnp.dot(w2.astype(BF), v_ref[...], preferred_element_type=F32)
        o4[rr, :] = (out / total).astype(BF)

    for g in range(4):
        o_ref[:, g * HD:(g + 1) * HD] = o4[g * 128:(g + 1) * 128, :]


def attention_call(owner_of, lengths, q, k, v, pre):
    return pl.pallas_call(
        attention_kernel,
        out_shape=jax.ShapeDtypeStruct((ROWS, 512), BF),
        grid_spec=pltpu.PrefetchScalarGridSpec(
            num_scalar_prefetch=2,
            grid=(4,),
            in_specs=[
                pl.BlockSpec((128, 512), lambda r, o, n: (r, 0)),
                pl.BlockSpec((128, HD), lambda r, o, n: (r, 0)),
                pl.BlockSpec((128, HD), lambda r, o, n: (r, 0)),
                pl.BlockSpec((1, 2, PREFIX, HD), lambda r, o, n: (o[r], 0, 0, 0)),
            ],
            out_specs=pl.BlockSpec((128, 512), lambda r, o, n: (r, 0)),
            scratch_shapes=[pltpu.VMEM((512, HD), BF), pltpu.VMEM((512, HD), BF)],
        ),
        compiler_params=pltpu.CompilerParams(vmem_limit_bytes=48 << 20),
        name="attend",
    )(owner_of, lengths, q, k, v, pre)


S_B1, S_A1, S_A2, S_B2 = (0, SB), (SB, SA), (256, SA), (256 + SA, SB)
N_SCATTER = 28


def scatter_kernel(att, wout, out, wv, part, rc, rf, rd, rz, bz, bc, bf, bd, send_sems, recv_sems, loc):
    p = places()
    x, zl, oz = p["x"], p["zl"], p["oz"]
    m = Mail(send_sems, recv_sems)
    order = [(2, 1), (2, 0), (1, 1), (3, 1), (1, 0), (3, 0), (0, 1), (0, 0)]

    def index(dx, dz):
        return ((x + dx) % 4) * 2 + (oz if dz else zl)

    weights = []
    for i, (dx, dz) in enumerate(order):
        c = pltpu.make_async_copy(
            wout.at[:, pl.ds(pl.multiple_of(index(dx, dz) * FEAT, FEAT), FEAT)], wv.at[i], loc.at[i])
        c.start()
        weights.append(c)
    barrier([p[k] for k in ("xp", "xm", "zp")])

    def slot(dx, dz, rows):
        return part.at[dx * 2 + dz, pl.ds(rows[0], rows[1])]

    def compute(i):
        dx, dz = order[i]
        weights[i].wait()

        @pl.loop(0, 2)
        def _(h):
            rr = pl.ds(pl.multiple_of(h * 256, 256), 256)
            part[dx * 2 + dz, rr, :] = jnp.dot(
                att[rr, :], wv[i], preferred_element_type=F32).astype(BF)

    def z_send(dx):
        m.send("z%d1" % dx, slot(dx, 1, S_B1), bz.at[dx, 0], p["zp"])
        m.send("z%d2" % dx, slot(dx, 1, S_B2), bz.at[dx, 1], p["zp"])

    compute(0)
    m.send("c11", slot(2, 1, S_A1), rc.at[1, 0], p["xm"])
    m.send("c12", slot(2, 1, S_A2), rc.at[1, 1], p["xp"])
    z_send(2)
    compute(1)
    m.send("c01", slot(2, 0, S_A1), rc.at[0, 0], p["xm"])
    m.send("c02", slot(2, 0, S_A2), rc.at[0, 1], p["xp"])
    compute(2)
    z_send(1)
    m.send("d11", slot(1, 1, S_A1), rd.at[1, 0], p["xp"])
    compute(3)
    z_send(3)
    m.send("d12", slot(3, 1, S_A2), rd.at[1, 1], p["xm"])
    compute(4)
    compute(5)
    compute(6)
    z_send(0)
    compute(7)

    def add_in(dx, dz, rows, got):
        s = slot(dx, dz, rows)
        s[...] = (s[...].astype(F32) + got[...].astype(F32)).astype(BF)

    for dz in (1, 0):
        m.recv("c%d1" % dz)
        add_in(3, dz, S_A1, rc.at[dz, 0])
        m.send("f%d1" % dz, slot(3, dz, S_A1), rf.at[dz, 0], p["xm"])
        m.recv("c%d2" % dz)
        add_in(1, dz, S_A2, rc.at[dz, 1])
        m.send("f%d2" % dz, slot(1, dz, S_A2), rf.at[dz, 1], p["xp"])
    m.send("d01", slot(1, 0, S_A1), rd.at[0, 0], p["xp"])
    m.send("d02", slot(3, 0, S_A2), rd.at[0, 1], p["xm"])
    m.recv("z21", "z22")
    add_in(2, 0, S_B1, bz.at[2, 0])
    m.send("bc1", slot(2, 0, S_B1), bc.at[0], p["xm"])
    add_in(2, 0, S_B2, bz.at[2, 1])
    m.send("bc2", slot(2, 0, S_B2), bc.at[1], p["xp"])
    m.recv("z11", "z12", "z31", "z32")
    add_in(1, 0, S_B1, bz.at[1, 0])
    m.send("bd1", slot(1, 0, S_B1), bd.at[0], p["xp"])
    add_in(3, 0, S_B2, bz.at[3, 1])
    m.send("bd2", slot(3, 0, S_B2), bd.at[1], p["xm"])
    add_in(1, 0, S_B2, bz.at[1, 1])
    add_in(3, 0, S_B1, bz.at[3, 0])
    m.recv("f11", "d11")
    s = slot(0, 1, S_A1)
    s[...] = (s[...].astype(F32) + rf[1, 0].astype(F32) + rd[1, 0].astype(F32)).astype(BF)
    m.send("e1", s, rz.at[0], p["zp"])
    m.recv("f12", "d12")
    s = slot(0, 1, S_A2)
    s[...] = (s[...].astype(F32) + rf[1, 1].astype(F32) + rd[1, 1].astype(F32)).astype(BF)
    m.send("e2", s, rz.at[1], p["zp"])
    m.recv("bc1")
    add_in(3, 0, S_B1, bc.at[0])
    m.send("bf1", slot(3, 0, S_B1), bf.at[0], p["xm"])
    m.recv("bc2")
    add_in(1, 0, S_B2, bc.at[1])
    m.send("bf2", slot(1, 0, S_B2), bf.at[1], p["xp"])
    for i, rows in ((0, S_A1), (1, S_A2)):
        m.recv("f0%d" % (i + 1), "d0%d" % (i + 1), "e%d" % (i + 1))
        total = slot(0, 0, rows)[...].astype(F32) + rf[0, i].astype(F32)
        total += rd[0, i].astype(F32) + rz[i].astype(F32)
        out[pl.ds(rows[0], rows[1]), :] = total
    m.recv("z01", "z02")
    for i, rows in ((0, S_B1), (1, S_B2)):
        m.recv("bf%d" % (i + 1), "bd%d" % (i + 1))
        total = slot(0, 0, rows)[...].astype(F32) + bz[0, i].astype(F32)
        total += bf[i].astype(F32) + bd[i].astype(F32)
        out[pl.ds(rows[0], rows[1]), :] = total
    m.drain()
    assert len(m.made) == N_SCATTER, len(m.made)


def scatter_call(att, wout):
    vm, hbm = pl.BlockSpec(memory_space=pltpu.VMEM), pl.BlockSpec(memory_space=pl.ANY)
    return pl.pallas_call(
        scatter_kernel,
        out_shape=jax.ShapeDtypeStruct((ROWS, FEAT), F32),
        in_specs=[vm, hbm],
        out_specs=vm,
        scratch_shapes=[
            pltpu.VMEM((8, 512, FEAT), BF),
            pltpu.VMEM((8, ROWS, FEAT), BF),
            pltpu.VMEM((2, 2, SA, FEAT), BF),
            pltpu.VMEM((2, 2, SA, FEAT), BF),
            pltpu.VMEM((2, 2, SA, FEAT), BF),
            pltpu.VMEM((2, SA, FEAT), BF),
            pltpu.VMEM((4, 2, SB, FEAT), BF),
            pltpu.VMEM((2, SB, FEAT), BF),
            pltpu.VMEM((2, SB, FEAT), BF),
            pltpu.VMEM((2, SB, FEAT), BF),
            pltpu.SemaphoreType.DMA((N_SCATTER,)),
            pltpu.SemaphoreType.DMA((N_SCATTER,)),
            pltpu.SemaphoreType.DMA((8,)),
        ],
        compiler_params=pltpu.CompilerParams(
            collective_id=1, has_side_effects=True, vmem_limit_bytes=56 << 20),
        name="scatter",
    )(att, wout)


def shards(hidden, norm_gain, w_query, w_kv, w_out, prefix_cache, lengths, groups, owners):
    n_req, suffix_len, feat = hidden.shape
    cos, sin = rope_tables(suffix_len, HD)
    q, k, v, prefixes = gather_call(
        hidden.reshape(ROWS, FEAT),
        prefix_cache.reshape(2 * PREFIX, HD),
        w_query,
        w_kv.reshape(16 * FEAT, HD),
        norm_gain.reshape(8, 1, FEAT),
        cos, sin)
    my_index = lax.axis_index("req")
    local_groups = lax.dynamic_slice_in_dim(groups, my_index * n_req, n_req)
    owner_of = jnp.sum(
        jnp.where(local_groups[:, None] == jnp.arange(16)[None, :], owners[None, :], 0), axis=-1)
    attention = attention_call(owner_of, lengths, q, k, v, prefixes)
    summed = scatter_call(attention, w_out)
    live = jnp.arange(suffix_len)[None, :] < lengths[:, None]
    mixed = hidden.astype(F32) + summed.reshape(n_req, suffix_len, feat)
    out_hidden = jnp.where(live[:, :, None], mixed, 0.0).astype(BF)
    kv = jnp.stack([k.reshape(n_req, suffix_len, HD), v.reshape(n_req, suffix_len, HD)], axis=2)
    suffix_cache = jnp.where(live[:, :, None, None], kv, jnp.zeros_like(kv))
    return out_hidden, suffix_cache


def solution(mesh):
    return jax.shard_map(
        shards,
        mesh=mesh,
        in_specs=(
            P("req", None, "tp"),
            P(),
            P(None, "tp"),
            P(None, None, "tp"),
            P("tp", None),
            P("req", None, None, "tp"),
            P("req"),
            P(),
            P(),
        ),
        out_specs=(P("req", None, "tp"), P("req", None, None, "tp")),
        check_vma=False,
    )
```

```python
import jax
import jax.numpy as jnp
import numpy as np
from jax import lax
from jax.experimental import pallas as pl
from jax.experimental.pallas import tpu as pltpu
from jax.sharding import PartitionSpec as P

PREFIX = 2048
EPSILON = 1e-05
ROPE_BASE = 5000000.0
MESH = pl.DeviceIdType.MESH
BF = jnp.bfloat16
F32 = jnp.float32

ROWS = 512
FEAT = 896
HD = 128


PSPLIT = 1536
PA, PB, PW = (0, PSPLIT), (PSPLIT, PREFIX - PSPLIT), (0, PREFIX)
H1, H2 = (0, 256), (256, 256)
CHUNKS = ((0, 32, 32), (128, 80, 112))
N_MAIL = 60 + 2 * 28


def rope_tables():
    f = np.float32
    positions = (PREFIX + np.arange(128)).astype(f)
    inverse = (f(ROPE_BASE) ** (-(f(2.0) * np.arange(HD // 2).astype(f)) / f(HD))).astype(f)
    angles = positions[:, None] * inverse[None, :]
    cosine = np.concatenate([np.cos(angles), np.cos(angles)], axis=-1)
    sine = np.concatenate([-np.sin(angles), np.sin(angles)], axis=-1)
    return cosine.astype(f), sine.astype(f)


def places():
    req, tp = lax.axis_index("req"), lax.axis_index("tp")
    x, zl = tp // 2, tp % 2
    y, low = req // 4, req % 4
    zh, core = low // 2, low % 2
    other_z = 1 - zl

    def at(xx, zz):
        return {"req": req, "tp": xx * 2 + zz}

    def own(yy, hh, cc):
        return {"req": yy * 4 + hh * 2 + cc, "tp": tp}

    return dict(
        req=req, tp=tp, x=x, zl=zl, y=y, zh=zh, core=core, oz=other_z,
        xp=at((x + 1) % 4, zl), xm=at((x + 3) % 4, zl), zp=at(x, other_z),
        yp=own((y + 1) % 4, zh, core), ym=own((y + 3) % 4, zh, core),
        zz=own(y, 1 - zh, core), cc=own(y, zh, 1 - core),
    )


class Mail:
    def __init__(self, send_sems, recv_sems):
        self.send_sems, self.recv_sems, self.made, self.left = send_sems, recv_sems, {}, []

    def send(self, name, src, dst, device):
        i = len(self.made)
        c = pltpu.make_async_remote_copy(
            src_ref=src, dst_ref=dst, send_sem=self.send_sems.at[i], recv_sem=self.recv_sems.at[i],
            device_id=device, device_id_type=MESH)
        c.start()
        self.made[name] = c
        self.left.append(c)

    def recv(self, *names):
        for name in names:
            self.made[name].wait_recv()

    def drain(self):
        for c in self.left:
            c.wait_send()
        self.left = []


class Part:
    def __init__(self, chunk, refs):
        first, b, a = chunk
        self.first, self.rows = first, 2 * (a + b)
        self.b1, self.a1 = (first, b), (first + b, a)
        self.a2, self.b2 = (first + b + a, a), (first + b + 2 * a, b)
        self.rc, self.rf, self.rd, self.rz, self.bz, self.bc, self.bf, self.bd = refs


def kernel(lens, groups, owners, hid, pre, wq, wkv, wout, gain, cos, sin, out, cache,
           xbuf, wq_v, wkv_v, wv, wf, wkvd, hown, praw, pref, acc, sq, q4, ks, vs, att, *rest):
    chunks = [Part(c, rest[8 * i:8 * i + 8]) for i, c in enumerate(CHUNKS)]
    send_sems, recv_sems, loc = rest[8 * len(CHUNKS):]
    p = places()
    req, tp, x, zl, oz = p["req"], p["tp"], p["x"], p["zl"], p["oz"]
    y, zh, core = p["y"], p["zh"], p["core"]
    peers = [p[k] for k in ("xp", "xm", "zp", "yp", "ym", "zz", "cc")]
    gate = pltpu.get_barrier_semaphore()
    for d in peers:
        pl.semaphore_signal(gate, inc=1, device_id=d, device_id_type=MESH)
    m = Mail(send_sems, recv_sems)

    def local(src, dst, i):
        c = pltpu.make_async_copy(src, dst, loc.at[i])
        c.start()
        return c

    def rows(ref, part):
        return ref.at[pl.ds(part[0], part[1])]

    def shard(dx, zz, part):
        return rows(xbuf.at[((x + dx) % 4) * 2 + zz], part)

    cp_pre = local(pre, praw, 0)
    cp_x = local(hid, xbuf.at[tp], 1)
    cp_wq = local(wq, wq_v, 2)
    cp_wkv = local(wkv, wkv_v, 3)
    cp_h = local(hid, hown, 4)

    mine = y * 4 + zh * 2 + core
    cp_pre.wait()

    @pl.loop(0, 4)
    def _(i):
        wf[pl.ds(0, 1024), :] = praw[pl.ds(pl.multiple_of(i * 1024, 1024), 1024), :].astype(F32)
        at = pl.ds(pl.multiple_of(i * 512, 512), 512)
        pref[mine, 0, at, :] = wf[pl.ds(0, 512, stride=2), :].astype(BF)
        pref[mine, 1, at, :] = wf[pl.ds(1, 512, stride=2), :].astype(BF)

    pl.semaphore_wait(gate, len(peers))

    def item(dy, side, kv, part):
        hh = (1 - zh) if side else zh
        return rows(pref.at[((y + dy) % 4) * 4 + hh * 2 + core, kv], part)

    def put(name, dy, side, kv, part, key):
        r = item(dy, side, kv, part)
        m.send(name, r, r, p[key])

    def give(name, dx, zz, part, key):
        r = shard(dx, zz, part)
        m.send(name, r, r, p[key])

    def own(name, part, key):
        m.send(name, rows(hid, part), shard(0, zl, part), p[key])

    own("z1", H1, "zp")
    own("xp1", H1, "xp")
    own("xm2", H2, "xm")
    put("ypK", 0, 0, 0, PW, "yp")
    put("ymV", 0, 0, 1, PW, "ym")
    own("z2", H2, "zp")
    own("xp2", H2, "xp")
    own("xm1", H1, "xm")
    put("ypV", 0, 0, 1, PW, "yp")
    put("ymK", 0, 0, 0, PW, "ym")
    put("zKA", 0, 0, 0, PA, "zz")
    put("zVA", 0, 0, 1, PA, "zz")
    put("zKB", 0, 0, 0, PB, "zz")
    put("zVB", 0, 0, 1, PB, "zz")
    put("C0", 0, 0, 0, PW, "cc")
    put("C1", 0, 0, 1, PW, "cc")

    acc[...] = jnp.zeros_like(acc)
    sq[...] = jnp.zeros_like(sq)

    def compute(first, count, step, zz):
        @pl.loop(0, count)
        def _(j):
            s = ((x + first + step * j) % 4) * 2 + zz
            at = pl.multiple_of(s * FEAT, FEAT)
            wf[...] = wkv_v[pl.ds(pl.multiple_of(s * 2 * FEAT, 2 * FEAT), 2 * FEAT), :].astype(F32)
            wkvd[:, 0:HD] = wf[pl.ds(0, FEAT, stride=2), :].astype(BF)
            wkvd[:, HD:2 * HD] = wf[pl.ds(1, FEAT, stride=2), :].astype(BF)
            g = gain[s]

            @pl.loop(0, 2)
            def _(h):
                rr = pl.ds(pl.multiple_of(h * 256, 256), 256)
                xv = xbuf[s, rr, :].astype(F32)
                x2 = xv * xv
                t = x2[:, 0:128]
                for b in range(1, FEAT // 128):
                    t += x2[:, b * 128:(b + 1) * 128]
                sq[rr, :] += t
                xg = (xv * g).astype(BF)
                acc[rr, 0:512] += jnp.dot(xg, wq_v[pl.ds(at, FEAT), :], preferred_element_type=F32)
                acc[rr, 512:768] += jnp.dot(xg, wkvd[...], preferred_element_type=F32)

    cp_x.wait()
    cp_wq.wait()
    cp_wkv.wait()
    compute(0, 1, 1, zl)

    m.recv("xp1")
    give("fx1", 3, zl, H1, "xp")
    m.recv("xm2")
    give("fx2", 1, zl, H2, "xm")
    m.recv("ypK")
    put("fyK", 3, 0, 0, PW, "yp")
    put("zbK3", 3, 0, 0, PB, "zz")
    put("C2", 3, 0, 0, PW, "cc")
    m.recv("ymV")
    put("fyV", 1, 0, 1, PW, "ym")
    put("zbV1", 1, 0, 1, PB, "zz")
    put("C3", 1, 0, 1, PW, "cc")
    m.recv("z1")
    give("pxp1", 0, oz, H1, "xp")
    m.recv("z2")
    give("pxm2", 0, oz, H2, "xm")
    give("pxp2", 0, oz, H2, "xp")
    give("pxm1", 0, oz, H1, "xm")
    m.recv("xp2", "xm1")
    m.recv("ypV", "ymK")
    put("zbV3", 3, 0, 1, PB, "zz")
    put("zbK1", 1, 0, 0, PB, "zz")
    put("C4", 3, 0, 1, PW, "cc")
    put("C5", 1, 0, 0, PW, "cc")
    compute(3, 2, 2, zl)
    m.recv("zKA")
    put("zypK", 0, 1, 0, PA, "yp")
    put("zymK", 0, 1, 0, PA, "ym")
    put("C6", 0, 1, 0, PA, "cc")
    m.recv("fx1", "fx2")
    m.recv("fyK", "fyV")
    put("zbK2", 2, 0, 0, PB, "zz")
    put("zbV2", 2, 0, 1, PB, "zz")
    put("C7", 2, 0, 0, PW, "cc")
    put("C8", 2, 0, 1, PW, "cc")
    m.recv("zVA")
    put("zymV", 0, 1, 1, PA, "ym")
    put("zypV", 0, 1, 1, PA, "yp")
    put("C9", 0, 1, 1, PA, "cc")
    compute(2, 1, 1, zl)
    m.recv("pxp1")
    give("fpx1", 3, oz, H1, "xp")
    m.recv("pxm2")
    give("fpx2", 1, oz, H2, "xm")
    compute(0, 1, 1, oz)
    m.recv("zypK")
    put("fzK", 3, 1, 0, PA, "yp")
    put("C10", 3, 1, 0, PA, "cc")
    m.recv("zymV")
    put("fzV", 1, 1, 1, PA, "ym")
    put("C11", 1, 1, 1, PA, "cc")
    m.recv("zKB", "zVB")
    put("C12", 0, 1, 0, PB, "cc")
    put("C13", 0, 1, 1, PB, "cc")
    m.recv("zbK3", "zbV1")
    put("C14", 3, 1, 0, PB, "cc")
    put("C15", 1, 1, 1, PB, "cc")
    m.recv("pxp2", "pxm1")
    compute(3, 2, 2, oz)
    m.recv("zbV3", "zbK1")
    put("C16", 3, 1, 1, PB, "cc")
    put("C17", 1, 1, 0, PB, "cc")
    m.recv("zypV", "zymK")
    put("C18", 3, 1, 1, PA, "cc")
    put("C19", 1, 1, 0, PA, "cc")
    m.recv("fpx1", "fpx2")
    order = [(2, 1), (2, 0), (1, 1), (3, 1), (1, 0), (3, 0), (0, 1), (0, 0)]

    def index(dx, dz):
        return ((x + dx) % 4) * 2 + (oz if dz else zl)

    weights = [
        local(wout.at[:, pl.ds(pl.multiple_of(index(dx, dz) * FEAT, FEAT), FEAT)], wv.at[i], 5 + i)
        for i, (dx, dz) in enumerate(order)]
    compute(2, 1, 1, oz)
    c, s = cos[...], sin[...]

    def finish(r):
        rr = slice(r * 128, (r + 1) * 128)
        mean = jnp.sum(sq[rr, :], axis=-1, keepdims=True) * (1.0 / (8 * FEAT))
        scale = lax.rsqrt(mean + EPSILON)
        for g in range(4):
            v = acc[rr, g * HD:(g + 1) * HD] * scale
            q4[r, g * 128:(g + 1) * 128, :] = (v * c + pltpu.roll(v, HD // 2, 1) * s).astype(BF)
        v = acc[rr, 512:640] * scale
        k = v * c + pltpu.roll(v, HD // 2, 1) * s
        v = acc[rr, 640:768] * scale
        ks[r] = k.astype(BF)
        vs[r] = v.astype(BF)
        wf[pl.ds(0, 128, stride=2), :] = k
        wf[pl.ds(1, 128, stride=2), :] = v
        live = lax.broadcasted_iota(jnp.int32, (256, HD), 0) // 2 < lens[r]
        cache[r * 256:(r + 1) * 256, :] = jnp.where(live, wf[0:256, :], 0.0).astype(BF)

    finish(0)
    m.recv("zbK2", "zbV2")
    put("C20", 2, 1, 0, PB, "cc")
    put("C21", 2, 1, 1, PB, "cc")
    m.recv("fzK")
    put("C22", 2, 1, 0, PA, "cc")
    m.recv("fzV")
    put("C23", 2, 1, 1, PA, "cc")
    m.drain()
    for i in range(24):
        m.recv("C%d" % i)

    factor = (HD ** -0.5) * 1.4426950408889634
    contract = (((1,), (1,)), ((), ()))

    def attend(r):
        slot = owners[groups[req * 4 + r]]
        length = lens[r]

        @pl.loop(0, 2)
        def _(i):
            q = q4[r, pl.ds(pl.multiple_of(i * 256, 256), 256), :]
            s1 = lax.dot_general(q, pref[slot, 0], contract, preferred_element_type=F32)
            s2 = lax.dot_general(q, ks[r], contract, preferred_element_type=F32)
            t = lax.broadcasted_iota(jnp.int32, (256, 128), 0) % 128
            pos = lax.broadcasted_iota(jnp.int32, (256, 128), 1)
            s2 = jnp.where((pos <= t) & (pos < length), s2, -jnp.inf)
            top = jnp.maximum(jnp.max(s1, axis=-1, keepdims=True), jnp.max(s2, axis=-1, keepdims=True))
            w1 = jnp.exp2((s1 - top) * factor)
            w2 = jnp.exp2((s2 - top) * factor)
            total = jnp.sum(w1, axis=-1, keepdims=True) + jnp.sum(w2, axis=-1, keepdims=True)
            o = jnp.dot(w1.astype(BF), pref[slot, 1], preferred_element_type=F32)
            o += jnp.dot(w2.astype(BF), vs[r], preferred_element_type=F32)
            o = (o / total).astype(BF)
            for j in range(2):
                lanes = pl.ds(pl.multiple_of((2 * i + j) * HD, HD), HD)
                att[r * 128:(r + 1) * 128, lanes] = o[j * 128:(j + 1) * 128, :]

    def slot(dx, dz, part):
        return xbuf.at[dx * 2 + dz, pl.ds(part[0], part[1])]

    def project(ch, i):
        dx, dz = order[i]
        if ch is chunks[0]:
            weights[i].wait()
        rr = slice(ch.first, ch.first + ch.rows)
        xbuf[dx * 2 + dz, rr, :] = jnp.dot(
            att[rr, :], wv[i], preferred_element_type=F32).astype(BF)

    def add_in(ref, *got):
        total = ref[...].astype(F32)
        for g in got:
            total += g[...].astype(F32)
        ref[...] = total.astype(BF)

    def stage1(n):
        ch = chunks[n]

        def z_send(dx):
            m.send("%dz%d1" % (n, dx), slot(dx, 1, ch.b1), ch.bz.at[dx, 0], p["zp"])
            m.send("%dz%d2" % (n, dx), slot(dx, 1, ch.b2), ch.bz.at[dx, 1], p["zp"])

        project(ch, 0)
        m.send("%dc11" % n, slot(2, 1, ch.a1), ch.rc.at[1, 0], p["xm"])
        m.send("%dc12" % n, slot(2, 1, ch.a2), ch.rc.at[1, 1], p["xp"])
        z_send(2)
        project(ch, 1)
        m.send("%dc01" % n, slot(2, 0, ch.a1), ch.rc.at[0, 0], p["xm"])
        m.send("%dc02" % n, slot(2, 0, ch.a2), ch.rc.at[0, 1], p["xp"])
        project(ch, 2)
        z_send(1)
        m.send("%dd11" % n, slot(1, 1, ch.a1), ch.rd.at[1, 0], p["xp"])
        project(ch, 3)
        z_send(3)
        m.send("%dd12" % n, slot(3, 1, ch.a2), ch.rd.at[1, 1], p["xm"])
        project(ch, 4)
        project(ch, 5)
        project(ch, 6)
        z_send(0)
        project(ch, 7)

    def stage2(n):
        ch = chunks[n]
        for dz in (1, 0):
            m.recv("%dc%d1" % (n, dz))
            add_in(slot(3, dz, ch.a1), ch.rc.at[dz, 0])
            m.send("%df%d1" % (n, dz), slot(3, dz, ch.a1), ch.rf.at[dz, 0], p["xm"])
            m.recv("%dc%d2" % (n, dz))
            add_in(slot(1, dz, ch.a2), ch.rc.at[dz, 1])
            m.send("%df%d2" % (n, dz), slot(1, dz, ch.a2), ch.rf.at[dz, 1], p["xp"])
        m.send("%dd01" % n, slot(1, 0, ch.a1), ch.rd.at[0, 0], p["xp"])
        m.send("%dd02" % n, slot(3, 0, ch.a2), ch.rd.at[0, 1], p["xm"])
        m.recv("%dz21" % n, "%dz22" % n)
        add_in(slot(2, 0, ch.b1), ch.bz.at[2, 0])
        m.send("%dbc1" % n, slot(2, 0, ch.b1), ch.bc.at[0], p["xm"])
        add_in(slot(2, 0, ch.b2), ch.bz.at[2, 1])
        m.send("%dbc2" % n, slot(2, 0, ch.b2), ch.bc.at[1], p["xp"])
        m.recv("%dz11" % n, "%dz12" % n, "%dz31" % n, "%dz32" % n)
        add_in(slot(1, 0, ch.b1), ch.bz.at[1, 0])
        m.send("%dbd1" % n, slot(1, 0, ch.b1), ch.bd.at[0], p["xp"])
        add_in(slot(3, 0, ch.b2), ch.bz.at[3, 1])
        m.send("%dbd2" % n, slot(3, 0, ch.b2), ch.bd.at[1], p["xm"])
        add_in(slot(1, 0, ch.b2), ch.bz.at[1, 1])
        add_in(slot(3, 0, ch.b1), ch.bz.at[3, 0])

    def stage3(n):
        ch = chunks[n]
        m.recv("%df11" % n, "%dd11" % n)
        add_in(slot(0, 1, ch.a1), ch.rf.at[1, 0], ch.rd.at[1, 0])
        m.send("%de1" % n, slot(0, 1, ch.a1), ch.rz.at[0], p["zp"])
        m.recv("%df12" % n, "%dd12" % n)
        add_in(slot(0, 1, ch.a2), ch.rf.at[1, 1], ch.rd.at[1, 1])
        m.send("%de2" % n, slot(0, 1, ch.a2), ch.rz.at[1], p["zp"])
        m.recv("%dbc1" % n)
        add_in(slot(3, 0, ch.b1), ch.bc.at[0])
        m.send("%dbf1" % n, slot(3, 0, ch.b1), ch.bf.at[0], p["xm"])
        m.recv("%dbc2" % n)
        add_in(slot(1, 0, ch.b2), ch.bc.at[1])
        m.send("%dbf2" % n, slot(1, 0, ch.b2), ch.bf.at[1], p["xp"])

    def result(part, *got):
        first, end = part[0], part[0] + part[1]
        while first < end:
            r = first // 128
            stop = min(end, (r + 1) * 128)
            size = stop - first
            total = hown[first:stop, :].astype(F32)
            terms = slot(0, 0, (first, size))[...].astype(F32)
            for g in got:
                terms += g[pl.ds(first - part[0], size), :].astype(F32)
            live = lax.broadcasted_iota(jnp.int32, (size, FEAT), 0) + (first - r * 128) < lens[r]
            out[first:stop, :] = jnp.where(live, total + terms, 0.0).astype(BF)
            first = stop

    def stage4(n):
        ch = chunks[n]
        for i, part in ((0, ch.a1), (1, ch.a2)):
            m.recv("%df0%d" % (n, i + 1), "%dd0%d" % (n, i + 1), "%de%d" % (n, i + 1))
            result(part, ch.rf.at[0, i], ch.rd.at[0, i], ch.rz.at[i])
        m.recv("%dz01" % n, "%dz02" % n)
        for i, part in ((0, ch.b1), (1, ch.b2)):
            m.recv("%dbf%d" % (n, i + 1), "%dbd%d" % (n, i + 1))
            result(part, ch.bz.at[0, i], ch.bf.at[i], ch.bd.at[i])

    attend(0)
    stage1(0)
    finish(1)
    attend(1)
    stage2(0)
    finish(2)
    attend(2)
    stage3(0)
    finish(3)
    attend(3)
    stage1(1)
    cp_h.wait()
    stage4(0)
    stage2(1)
    stage3(1)
    stage4(1)
    m.drain()
    assert len(m.made) == N_MAIL, len(m.made)


def shards(hidden, norm_gain, w_query, w_kv, w_out, prefix_cache, lengths, groups, owners):
    n_req, suffix_len, feat = hidden.shape
    cos, sin = rope_tables()
    vm, hbm = pl.BlockSpec(memory_space=pltpu.VMEM), pl.BlockSpec(memory_space=pl.ANY)
    sm = pl.BlockSpec(memory_space=pltpu.SMEM)
    arrivals = []
    for _, b, a in CHUNKS:
        arrivals += [pltpu.VMEM((2, 2, a, FEAT), BF)] * 3 + [pltpu.VMEM((2, a, FEAT), BF)]
        arrivals += [pltpu.VMEM((4, 2, b, FEAT), BF)] + [pltpu.VMEM((2, b, FEAT), BF)] * 3
    out, cache = pl.pallas_call(
        kernel,
        out_shape=(
            jax.ShapeDtypeStruct((ROWS, FEAT), BF),
            jax.ShapeDtypeStruct((2 * ROWS, HD), BF),
        ),
        in_specs=[sm, sm, sm, hbm, hbm, hbm, hbm, hbm, vm, vm, vm],
        out_specs=(vm, vm),
        scratch_shapes=[
            pltpu.VMEM((8, ROWS, FEAT), BF),
            pltpu.VMEM((8 * FEAT, 512), BF),
            pltpu.VMEM((16 * FEAT, HD), BF),
            pltpu.VMEM((8, 512, FEAT), BF),
            pltpu.VMEM((2 * FEAT, HD), F32),
            pltpu.VMEM((FEAT, 2 * HD), BF),
            pltpu.VMEM((ROWS, FEAT), BF),
            pltpu.VMEM((2 * PREFIX, HD), BF),
            pltpu.VMEM((16, 2, PREFIX, HD), BF),
            pltpu.VMEM((ROWS, 768), F32),
            pltpu.VMEM((ROWS, HD), F32),
            pltpu.VMEM((4, 512, HD), BF),
            pltpu.VMEM((4, 128, HD), BF),
            pltpu.VMEM((4, 128, HD), BF),
            pltpu.VMEM((ROWS, 512), BF),
            *arrivals,
            pltpu.SemaphoreType.DMA((N_MAIL,)),
            pltpu.SemaphoreType.DMA((N_MAIL,)),
            pltpu.SemaphoreType.DMA((13,)),
        ],
        compiler_params=pltpu.CompilerParams(
            collective_id=0, has_side_effects=True, vmem_limit_bytes=67043328),
        name="layer",
    )(
        lengths, groups, owners,
        hidden.reshape(ROWS, FEAT),
        prefix_cache.reshape(2 * PREFIX, HD),
        w_query,
        w_kv.reshape(16 * FEAT, HD),
        w_out,
        norm_gain.reshape(8, 1, FEAT),
        cos, sin)
    return out.reshape(n_req, suffix_len, feat), cache.reshape(n_req, suffix_len, 2, HD)


def solution(mesh):
    return jax.shard_map(
        shards,
        mesh=mesh,
        in_specs=(
            P("req", None, "tp"),
            P(),
            P(None, "tp"),
            P(None, None, "tp"),
            P("tp", None),
            P("req", None, None, "tp"),
            P("req"),
            P(),
            P(),
        ),
        out_specs=(P("req", None, "tp"), P("req", None, None, "tp")),
        check_vma=False,
    )
```

```python
import jax
import jax.numpy as jnp
import numpy as np
from jax import lax
from jax.experimental import pallas as pl
from jax.experimental.pallas import tpu as pltpu
from jax.sharding import PartitionSpec as P

PREFIX = 2048
EPSILON = 1e-05
ROPE_BASE = 5000000.0
MESH = pl.DeviceIdType.MESH
BF = jnp.bfloat16
F32 = jnp.float32

ROWS = 512
FEAT = 896
HD = 128


PSPLIT = 1536
PA, PB, PW = (0, PSPLIT), (PSPLIT, PREFIX - PSPLIT), (0, PREFIX)
H1, H2 = (0, 256), (256, 256)
WROWS = 64
N_MAIL = 60 + 17 + 2 * 13 + 2 * 10


def rope_tables():
    f = np.float32
    positions = (PREFIX + np.arange(128)).astype(f)
    inverse = (f(ROPE_BASE) ** (-(f(2.0) * np.arange(HD // 2).astype(f)) / f(HD))).astype(f)
    angles = positions[:, None] * inverse[None, :]
    cosine = np.concatenate([np.cos(angles), np.cos(angles)], axis=-1)
    sine = np.concatenate([-np.sin(angles), np.sin(angles)], axis=-1)
    return cosine.astype(f), sine.astype(f)


def places():
    req, tp = lax.axis_index("req"), lax.axis_index("tp")
    x, zl = tp // 2, tp % 2
    y, low = req // 4, req % 4
    zh, core = low // 2, low % 2
    other_z = 1 - zl

    def at(xx, zz):
        return {"req": req, "tp": xx * 2 + zz}

    def own(yy, hh, cc):
        return {"req": yy * 4 + hh * 2 + cc, "tp": tp}

    return dict(
        req=req, tp=tp, x=x, zl=zl, y=y, zh=zh, core=core, oz=other_z,
        xp=at((x + 1) % 4, zl), xm=at((x + 3) % 4, zl), zp=at(x, other_z),
        yp=own((y + 1) % 4, zh, core), ym=own((y + 3) % 4, zh, core),
        zz=own(y, 1 - zh, core), cc=own(y, zh, 1 - core),
    )


class Mail:
    def __init__(self, send_sems, recv_sems):
        self.send_sems, self.recv_sems, self.made, self.left = send_sems, recv_sems, {}, []

    def send(self, name, src, dst, device):
        i = len(self.made)
        c = pltpu.make_async_remote_copy(
            src_ref=src, dst_ref=dst, send_sem=self.send_sems.at[i], recv_sem=self.recv_sems.at[i],
            device_id=device, device_id_type=MESH)
        c.start()
        self.made[name] = c
        self.left.append(c)

    def recv(self, *names):
        for name in names:
            self.made[name].wait_recv()

    def drain(self):
        for c in self.left:
            c.wait_send()
        self.left = []


def kernel(lens, groups, owners, hid, pre, wq, wkv, wout, gain, cos, sin, out, cache,
           xbuf, wq_v, wkv_v, wcol, wf, wkvd, hown, praw, pref, acc, sq, q4, ks, vs, ag, total,
           send_sems, recv_sems, loc):
    p = places()
    req, tp, x, zl, oz = p["req"], p["tp"], p["x"], p["zl"], p["oz"]
    y, zh, core = p["y"], p["zh"], p["core"]
    tp_peers = [{"req": req, "tp": (tp + d) % 8} for d in range(1, 8)]
    peers = tp_peers + [p[k] for k in ("yp", "ym", "zz", "cc")]
    gate = pltpu.get_barrier_semaphore()
    for d in peers:
        pl.semaphore_signal(gate, inc=1, device_id=d, device_id_type=MESH)
    m = Mail(send_sems, recv_sems)

    def local(src, dst, i):
        c = pltpu.make_async_copy(src, dst, loc.at[i])
        c.start()
        return c

    def rows(ref, part):
        return ref.at[pl.ds(part[0], part[1])]

    def shard(dx, zz, part):
        return rows(xbuf.at[((x + dx) % 4) * 2 + zz], part)

    cp_pre = local(pre, praw, 0)
    cp_x = local(hid, xbuf.at[tp], 1)
    cp_wq = local(wq, wq_v, 2)
    cp_wkv = local(wkv, wkv_v, 3)
    cp_h = local(hid, hown, 4)
    cp_w = local(wout.at[:, pl.ds(pl.multiple_of(tp * FEAT, FEAT), FEAT)], wcol.at[0], 5)

    mine = y * 4 + zh * 2 + core
    cp_pre.wait()

    @pl.loop(0, 4)
    def _(i):
        wf[pl.ds(0, 1024), :] = praw[pl.ds(pl.multiple_of(i * 1024, 1024), 1024), :].astype(F32)
        at = pl.ds(pl.multiple_of(i * 512, 512), 512)
        pref[mine, 0, at, :] = wf[pl.ds(0, 512, stride=2), :].astype(BF)
        pref[mine, 1, at, :] = wf[pl.ds(1, 512, stride=2), :].astype(BF)

    pl.semaphore_wait(gate, len(peers))

    def item(dy, side, kv, part):
        hh = (1 - zh) if side else zh
        return rows(pref.at[((y + dy) % 4) * 4 + hh * 2 + core, kv], part)

    def put(name, dy, side, kv, part, key):
        r = item(dy, side, kv, part)
        m.send(name, r, r, p[key])

    def give(name, dx, zz, part, key):
        r = shard(dx, zz, part)
        m.send(name, r, r, p[key])

    def own(name, part, key):
        m.send(name, rows(hid, part), shard(0, zl, part), p[key])

    own("z1", H1, "zp")
    own("xp1", H1, "xp")
    own("xm2", H2, "xm")
    put("ypK", 0, 0, 0, PW, "yp")
    put("ymV", 0, 0, 1, PW, "ym")
    own("z2", H2, "zp")
    own("xp2", H2, "xp")
    own("xm1", H1, "xm")
    put("ypV", 0, 0, 1, PW, "yp")
    put("ymK", 0, 0, 0, PW, "ym")
    put("zKA", 0, 0, 0, PA, "zz")
    put("zVA", 0, 0, 1, PA, "zz")
    put("zKB", 0, 0, 0, PB, "zz")
    put("zVB", 0, 0, 1, PB, "zz")
    put("C0", 0, 0, 0, PW, "cc")
    put("C1", 0, 0, 1, PW, "cc")

    acc[...] = jnp.zeros_like(acc)
    sq[...] = jnp.zeros_like(sq)

    def compute(first, count, step, zz):
        @pl.loop(0, count)
        def _(j):
            s = ((x + first + step * j) % 4) * 2 + zz
            at = pl.multiple_of(s * FEAT, FEAT)
            wf[...] = wkv_v[pl.ds(pl.multiple_of(s * 2 * FEAT, 2 * FEAT), 2 * FEAT), :].astype(F32)
            wkvd[:, 0:HD] = wf[pl.ds(0, FEAT, stride=2), :].astype(BF)
            wkvd[:, HD:2 * HD] = wf[pl.ds(1, FEAT, stride=2), :].astype(BF)
            g = gain[s]

            @pl.loop(0, 2)
            def _(h):
                rr = pl.ds(pl.multiple_of(h * 256, 256), 256)
                xv = xbuf[s, rr, :].astype(F32)
                x2 = xv * xv
                t = x2[:, 0:128]
                for b in range(1, FEAT // 128):
                    t += x2[:, b * 128:(b + 1) * 128]
                sq[rr, :] += t
                xg = (xv * g).astype(BF)
                acc[rr, 0:512] += jnp.dot(xg, wq_v[pl.ds(at, FEAT), :], preferred_element_type=F32)
                acc[rr, 512:768] += jnp.dot(xg, wkvd[...], preferred_element_type=F32)

    cp_x.wait()
    cp_wq.wait()
    cp_wkv.wait()
    compute(0, 1, 1, zl)

    m.recv("xp1")
    give("fx1", 3, zl, H1, "xp")
    m.recv("xm2")
    give("fx2", 1, zl, H2, "xm")
    m.recv("ypK")
    put("fyK", 3, 0, 0, PW, "yp")
    put("zbK3", 3, 0, 0, PB, "zz")
    put("C2", 3, 0, 0, PW, "cc")
    m.recv("ymV")
    put("fyV", 1, 0, 1, PW, "ym")
    put("zbV1", 1, 0, 1, PB, "zz")
    put("C3", 1, 0, 1, PW, "cc")
    m.recv("z1")
    give("pxp1", 0, oz, H1, "xp")
    m.recv("z2")
    give("pxm2", 0, oz, H2, "xm")
    give("pxp2", 0, oz, H2, "xp")
    give("pxm1", 0, oz, H1, "xm")
    m.recv("xp2", "xm1")
    m.recv("ypV", "ymK")
    put("zbV3", 3, 0, 1, PB, "zz")
    put("zbK1", 1, 0, 0, PB, "zz")
    put("C4", 3, 0, 1, PW, "cc")
    put("C5", 1, 0, 0, PW, "cc")
    compute(3, 2, 2, zl)
    m.recv("zKA")
    put("zypK", 0, 1, 0, PA, "yp")
    put("zymK", 0, 1, 0, PA, "ym")
    put("C6", 0, 1, 0, PA, "cc")
    m.recv("fx1", "fx2")
    m.recv("fyK", "fyV")
    put("zbK2", 2, 0, 0, PB, "zz")
    put("zbV2", 2, 0, 1, PB, "zz")
    put("C7", 2, 0, 0, PW, "cc")
    put("C8", 2, 0, 1, PW, "cc")
    m.recv("zVA")
    put("zymV", 0, 1, 1, PA, "ym")
    put("zypV", 0, 1, 1, PA, "yp")
    put("C9", 0, 1, 1, PA, "cc")
    compute(2, 1, 1, zl)
    m.recv("pxp1")
    give("fpx1", 3, oz, H1, "xp")
    m.recv("pxm2")
    give("fpx2", 1, oz, H2, "xm")
    piece = pl.multiple_of((y * 2 + core) * WROWS, WROWS)
    for d in (4, 2, 6, 1, 3, 5, 7):
        cols = pl.ds(pl.multiple_of((tp + d) % 8 * FEAT, FEAT), FEAT)
        m.send("w%d" % d, wout.at[pl.ds(piece, WROWS), cols], wcol.at[8 - d, pl.ds(piece, WROWS)],
               tp_peers[d - 1])
    compute(0, 1, 1, oz)
    m.recv("zypK")
    put("fzK", 3, 1, 0, PA, "yp")
    put("C10", 3, 1, 0, PA, "cc")
    m.recv("zymV")
    put("fzV", 1, 1, 1, PA, "ym")
    put("C11", 1, 1, 1, PA, "cc")
    m.recv("zKB", "zVB")
    put("C12", 0, 1, 0, PB, "cc")
    put("C13", 0, 1, 1, PB, "cc")
    m.recv("zbK3", "zbV1")
    put("C14", 3, 1, 0, PB, "cc")
    put("C15", 1, 1, 1, PB, "cc")
    m.recv("pxp2", "pxm1")
    compute(3, 2, 2, oz)
    m.recv("zbV3", "zbK1")
    put("C16", 3, 1, 1, PB, "cc")
    put("C17", 1, 1, 0, PB, "cc")
    m.recv("zypV", "zymK")
    put("C18", 3, 1, 1, PA, "cc")
    put("C19", 1, 1, 0, PA, "cc")
    m.recv("fpx1", "fpx2")
    compute(2, 1, 1, oz)
    c, s = cos[...], sin[...]

    def finish(r):
        rr = slice(r * 128, (r + 1) * 128)
        mean = jnp.sum(sq[rr, :], axis=-1, keepdims=True) * (1.0 / (8 * FEAT))
        scale = lax.rsqrt(mean + EPSILON)
        for g in range(4):
            v = acc[rr, g * HD:(g + 1) * HD] * scale
            q4[r, g * 128:(g + 1) * 128, :] = (v * c + pltpu.roll(v, HD // 2, 1) * s).astype(BF)
        v = acc[rr, 512:640] * scale
        k = v * c + pltpu.roll(v, HD // 2, 1) * s
        v = acc[rr, 640:768] * scale
        ks[r] = k.astype(BF)
        vs[r] = v.astype(BF)
        wf[pl.ds(0, 128, stride=2), :] = k
        wf[pl.ds(1, 128, stride=2), :] = v
        live = lax.broadcasted_iota(jnp.int32, (256, HD), 0) // 2 < lens[r]
        cache[r * 256:(r + 1) * 256, :] = jnp.where(live, wf[0:256, :], 0.0).astype(BF)

    finish(0)
    m.recv("zbK2", "zbV2")
    put("C20", 2, 1, 0, PB, "cc")
    put("C21", 2, 1, 1, PB, "cc")
    m.recv("fzK")
    put("C22", 2, 1, 0, PA, "cc")
    m.recv("fzV")
    put("C23", 2, 1, 1, PA, "cc")
    for i in range(24):
        m.recv("C%d" % i)

    factor = (HD ** -0.5) * 1.4426950408889634
    contract = (((1,), (1,)), ((), ()))

    def attend(r):
        slot = owners[groups[req * 4 + r]]
        length = lens[r]

        @pl.loop(0, 2)
        def _(i):
            q = q4[r, pl.ds(pl.multiple_of(i * 256, 256), 256), :]
            s1 = lax.dot_general(q, pref[slot, 0], contract, preferred_element_type=F32)
            s2 = lax.dot_general(q, ks[r], contract, preferred_element_type=F32)
            t = lax.broadcasted_iota(jnp.int32, (256, 128), 0) % 128
            pos = lax.broadcasted_iota(jnp.int32, (256, 128), 1)
            s2 = jnp.where((pos <= t) & (pos < length), s2, -jnp.inf)
            top = jnp.maximum(jnp.max(s1, axis=-1, keepdims=True), jnp.max(s2, axis=-1, keepdims=True))
            w1 = jnp.exp2((s1 - top) * factor)
            w2 = jnp.exp2((s2 - top) * factor)
            total = jnp.sum(w1, axis=-1, keepdims=True) + jnp.sum(w2, axis=-1, keepdims=True)
            o = jnp.dot(w1.astype(BF), pref[slot, 1], preferred_element_type=F32)
            o += jnp.dot(w2.astype(BF), vs[r], preferred_element_type=F32)
            o = (o / total).astype(BF)
            for j in range(2):
                lanes = pl.ds(pl.multiple_of((2 * i + j) * HD, HD), HD)
                ag[tp, r * 128:(r + 1) * 128, lanes] = o[j * 128:(j + 1) * 128, :]

    def rows_of(r):
        return (r * 128, 128), (r * 128, 64), (r * 128 + 64, 64)

    def pass_att(name, dx, zz, part, key):
        ref = rows(ag.at[((x + dx) % 4) * 2 + zz], part)
        m.send(name, ref, ref, p[key])

    def x_start(r, pre, zz):
        _, h1, h2 = rows_of(r)
        pass_att("%d%sxp1" % (r, pre), 0, zz, h1, "xp")
        pass_att("%d%sxm2" % (r, pre), 0, zz, h2, "xm")
        pass_att("%d%sxp2" % (r, pre), 0, zz, h2, "xp")
        pass_att("%d%sxm1" % (r, pre), 0, zz, h1, "xm")

    def x_forward(r, pre, zz):
        _, h1, h2 = rows_of(r)
        m.recv("%d%sxp1" % (r, pre))
        pass_att("%d%sfx1" % (r, pre), 3, zz, h1, "xp")
        m.recv("%d%sxm2" % (r, pre))
        pass_att("%d%sfx2" % (r, pre), 1, zz, h2, "xm")

    def x_near(r, pre):
        m.recv("%d%sxp2" % (r, pre), "%d%sxm1" % (r, pre))

    def x_far(r, pre):
        m.recv("%d%sfx1" % (r, pre), "%d%sfx2" % (r, pre))

    def z_pass(r, *shifts):
        for dx in shifts:
            pass_att("%dz%d" % (r, dx), dx, zl, rows_of(r)[0], "zp")

    def z_get(r, *shifts):
        m.recv(*["%dz%d" % (r, dx) for dx in shifts])

    def piece_of(dy, half, size):
        first = pl.multiple_of((((y + dy) % 4) * 2 + core) * WROWS + half * (WROWS // 2), WROWS // 2)
        return wcol.at[pl.ds(1, 7), pl.ds(first, size)]

    def pass_w(name, dy, half, key, size=WROWS // 2):
        ref = piece_of(dy, half, size)
        m.send(name, ref, ref, p[key])

    def project(r, first, count, step, zz):
        @pl.loop(0, count)
        def _(j):
            t = ((x + first + step * j) % 4) * 2 + zz
            rr = slice(r * 128, r * 128 + 256)
            total[rr, :] += jnp.dot(ag[t, rr, :], wcol[(t - tp + 8) % 8], preferred_element_type=F32)

    def result(r):
        rr = slice(r * 128, (r + 1) * 128)
        live = lax.broadcasted_iota(jnp.int32, (128, FEAT), 0) < lens[r]
        out[rr, :] = jnp.where(live, hown[rr, :].astype(F32) + total[rr, :], 0.0).astype(BF)

    attend(0)
    z_pass(0, 0)
    x_start(0, "", zl)
    total[...] = jnp.zeros_like(total)
    m.recv(*["w%d" % d for d in range(1, 8)])
    pass_w("wyp1", 0, 0, "yp")
    pass_w("wym2", 0, 1, "ym")
    pass_w("wyp2", 0, 1, "yp")
    pass_w("wym1", 0, 0, "ym")
    pass_w("D0", 0, 0, "cc", WROWS)
    finish(1)
    attend(1)
    x_start(1, "", zl)
    z_pass(1, 0)
    x_forward(0, "", zl)
    z_get(0, 0)
    x_start(0, "p", oz)
    finish(2)
    attend(2)
    z_pass(2, 0)
    x_start(2, "", zl)
    x_forward(1, "", zl)
    x_near(1, "")
    z_pass(1, 1, 3)
    x_forward(0, "p", oz)
    m.recv("wyp1")
    pass_w("wfx1", 3, 0, "yp")
    m.recv("wym2")
    pass_w("wfx2", 1, 1, "ym")
    finish(3)
    attend(3)
    x_start(3, "", zl)
    z_pass(3, 0)
    x_far(1, "")
    z_pass(1, 2)
    x_forward(2, "", zl)
    z_get(2, 0)
    x_start(2, "p", oz)
    x_forward(3, "", zl)
    x_near(3, "")
    z_pass(3, 1, 3)
    x_forward(2, "p", oz)
    x_far(3, "")
    z_pass(3, 2)
    m.recv("wyp2", "wym1")
    pass_w("D1", 3, 0, "cc", WROWS)
    pass_w("D2", 1, 0, "cc", WROWS)
    m.recv("wfx1", "wfx2")
    pass_w("D3", 2, 0, "cc", WROWS)
    cp_h.wait()
    cp_w.wait()
    m.recv("D0", "D1", "D2", "D3")
    x_near(0, "")
    x_far(0, "")
    project(0, 0, 4, 1, zl)
    x_near(0, "p")
    x_far(0, "p")
    z_get(1, 0, 1, 2, 3)
    project(0, 0, 4, 1, oz)
    x_near(2, "")
    x_far(2, "")
    project(2, 0, 4, 1, zl)
    result(0)
    result(1)
    x_near(2, "p")
    z_get(3, 0, 1, 3)
    project(2, 0, 2, 1, oz)
    project(2, 3, 1, 1, oz)
    x_far(2, "p")
    z_get(3, 2)
    project(2, 2, 1, 1, oz)
    result(2)
    result(3)
    m.drain()
    assert len(m.made) == N_MAIL, len(m.made)


def emit_kernel(a, b, oa, ob, va, vb, sems):
    n = 4
    jobs = [(a, va, oa, i * (ROWS // n), ROWS // n) for i in range(n)] + [(b, vb, ob, 0, 2 * ROWS)]
    ins = []
    for i, (src, mid, _, first, size) in enumerate(jobs):
        at = pl.ds(first, size)
        c = pltpu.make_async_copy(src.at[at], mid.at[at], sems.at[i])
        c.start()
        ins.append(c)
    outs = []
    for i, (_, mid, dst, first, size) in enumerate(jobs):
        at = pl.ds(first, size)
        ins[i].wait()
        c = pltpu.make_async_copy(mid.at[at], dst.at[at], sems.at[len(jobs) + i])
        c.start()
        outs.append(c)
    for c in outs:
        c.wait()


def emit(a, b):
    hbm = pl.BlockSpec(memory_space=pl.ANY)
    return pl.pallas_call(
        emit_kernel,
        out_shape=(jax.ShapeDtypeStruct(a.shape, BF), jax.ShapeDtypeStruct(b.shape, BF)),
        in_specs=[hbm, hbm],
        out_specs=(hbm, hbm),
        scratch_shapes=[pltpu.VMEM(a.shape, BF), pltpu.VMEM(b.shape, BF), pltpu.SemaphoreType.DMA((10,))],
        name="emit",
    )(a, b)


def shards(hidden, norm_gain, w_query, w_kv, w_out, prefix_cache, lengths, groups, owners):
    n_req, suffix_len, feat = hidden.shape
    cos, sin = rope_tables()
    vm, hbm = pl.BlockSpec(memory_space=pltpu.VMEM), pl.BlockSpec(memory_space=pl.ANY)
    sm = pl.BlockSpec(memory_space=pltpu.SMEM)
    out, cache = pl.pallas_call(
        kernel,
        out_shape=(
            jax.ShapeDtypeStruct((ROWS, FEAT), BF),
            jax.ShapeDtypeStruct((2 * ROWS, HD), BF),
        ),
        in_specs=[sm, sm, sm, hbm, hbm, hbm, hbm, hbm, vm, vm, vm],
        out_specs=(vm, vm),
        scratch_shapes=[
            pltpu.VMEM((8, ROWS, FEAT), BF),
            pltpu.VMEM((8 * FEAT, 512), BF),
            pltpu.VMEM((16 * FEAT, HD), BF),
            pltpu.VMEM((8, 512, FEAT), BF),
            pltpu.VMEM((2 * FEAT, HD), F32),
            pltpu.VMEM((FEAT, 2 * HD), BF),
            pltpu.VMEM((ROWS, FEAT), BF),
            pltpu.VMEM((2 * PREFIX, HD), BF),
            pltpu.VMEM((16, 2, PREFIX, HD), BF),
            pltpu.VMEM((ROWS, 768), F32),
            pltpu.VMEM((ROWS, HD), F32),
            pltpu.VMEM((4, 512, HD), BF),
            pltpu.VMEM((4, 128, HD), BF),
            pltpu.VMEM((4, 128, HD), BF),
            pltpu.VMEM((8, ROWS, 512), BF),
            pltpu.VMEM((ROWS, FEAT), F32),
            pltpu.SemaphoreType.DMA((N_MAIL,)),
            pltpu.SemaphoreType.DMA((N_MAIL,)),
            pltpu.SemaphoreType.DMA((6,)),
        ],
        compiler_params=pltpu.CompilerParams(
            collective_id=0, has_side_effects=True, vmem_limit_bytes=67043328),
        name="layer",
    )(
        lengths, groups, owners,
        hidden.reshape(ROWS, FEAT),
        prefix_cache.reshape(2 * PREFIX, HD),
        w_query,
        w_kv.reshape(16 * FEAT, HD),
        w_out,
        norm_gain.reshape(8, 1, FEAT),
        cos, sin)
    out, cache = emit(out, cache)
    return out.reshape(n_req, suffix_len, feat), cache.reshape(n_req, suffix_len, 2, HD)


def solution(mesh):
    return jax.shard_map(
        shards,
        mesh=mesh,
        in_specs=(
            P("req", None, "tp"),
            P(),
            P(None, "tp"),
            P(None, None, "tp"),
            P("tp", None),
            P("req", None, None, "tp"),
            P("req"),
            P(),
            P(),
        ),
        out_specs=(P("req", None, "tp"), P("req", None, None, "tp")),
        check_vma=False,
    )
```

```python
import jax
import jax.numpy as jnp
import numpy as np
from jax import lax
from jax.experimental import pallas as pl
from jax.experimental.pallas import tpu as pltpu
from jax.sharding import PartitionSpec as P

PREFIX = 2048
EPSILON = 1e-05
ROPE_BASE = 5000000.0
MESH = pl.DeviceIdType.MESH
BF = jnp.bfloat16
F32 = jnp.float32

ROWS = 512
FEAT = 896
HD = 128


PSPLIT = 1664
PA, PB, PW = (0, PSPLIT), (PSPLIT, PREFIX - PSPLIT), (0, PREFIX)
H1, H2 = (0, 256), (256, 256)
WROWS = 64
HALF = WROWS // 2
N_MAIL = 60 + 24 + 2 * 13 + 2 * 10


def rope_tables():
    f = np.float32
    positions = (PREFIX + np.arange(128)).astype(f)
    inverse = (f(ROPE_BASE) ** (-(f(2.0) * np.arange(HD // 2).astype(f)) / f(HD))).astype(f)
    angles = positions[:, None] * inverse[None, :]
    cosine = np.concatenate([np.cos(angles), np.cos(angles)], axis=-1)
    sine = np.concatenate([-np.sin(angles), np.sin(angles)], axis=-1)
    return cosine.astype(f), sine.astype(f)


def places():
    req, tp = lax.axis_index("req"), lax.axis_index("tp")
    x, zl = tp // 2, tp % 2
    y, low = req // 4, req % 4
    zh, core = low // 2, low % 2
    other_z = 1 - zl

    def at(xx, zz):
        return {"req": req, "tp": xx * 2 + zz}

    def own(yy, hh, cc):
        return {"req": yy * 4 + hh * 2 + cc, "tp": tp}

    return dict(
        req=req, tp=tp, x=x, zl=zl, y=y, zh=zh, core=core, oz=other_z,
        xp=at((x + 1) % 4, zl), xm=at((x + 3) % 4, zl), zp=at(x, other_z),
        yp=own((y + 1) % 4, zh, core), ym=own((y + 3) % 4, zh, core),
        zz=own(y, 1 - zh, core), cc=own(y, zh, 1 - core),
    )


class Mail:
    def __init__(self, send_sems, recv_sems):
        self.send_sems, self.recv_sems, self.made, self.left = send_sems, recv_sems, {}, []

    def send(self, name, src, dst, device):
        i = len(self.made)
        c = pltpu.make_async_remote_copy(
            src_ref=src, dst_ref=dst, send_sem=self.send_sems.at[i], recv_sem=self.recv_sems.at[i],
            device_id=device, device_id_type=MESH)
        c.start()
        self.made[name] = c
        self.left.append(c)

    def recv(self, *names):
        for name in names:
            self.made[name].wait_recv()

    def drain(self):
        for c in self.left:
            c.wait_send()
        self.left = []


def kernel(lens, groups, owners, hid, pre, wq, wkv, wout, gain, cos, sin, out, cache,
           out_v, cache_v, xbuf, wq_v, wkv_v, wcol, wf, wkvd, hown, praw, pref, acc, sq, q4, ks, vs, ag, total,
           send_sems, recv_sems, loc):
    p = places()
    req, tp, x, zl, oz = p["req"], p["tp"], p["x"], p["zl"], p["oz"]
    y, zh, core = p["y"], p["zh"], p["core"]
    tp_peers = [{"req": req, "tp": (tp + d) % 8} for d in range(1, 8)]
    peers = tp_peers + [p[k] for k in ("yp", "ym", "zz", "cc")]
    gate = pltpu.get_barrier_semaphore()
    for d in peers:
        pl.semaphore_signal(gate, inc=1, device_id=d, device_id_type=MESH)
    m = Mail(send_sems, recv_sems)

    def local(src, dst, i):
        c = pltpu.make_async_copy(src, dst, loc.at[i])
        c.start()
        return c

    def rows(ref, part):
        return ref.at[pl.ds(part[0], part[1])]

    def shard(dx, zz, part):
        return rows(xbuf.at[((x + dx) % 4) * 2 + zz], part)

    cp_pre = local(pre, praw, 0)
    cp_x = local(hid, xbuf.at[tp], 1)
    cp_wq = local(wq, wq_v, 2)
    cp_wkv = local(wkv, wkv_v, 3)
    cp_h = local(hid, hown, 4)
    cp_w = local(wout.at[:, pl.ds(pl.multiple_of(tp * FEAT, FEAT), FEAT)], wcol.at[0], 5)

    mine = y * 4 + zh * 2 + core
    cp_pre.wait()

    @pl.loop(0, 4)
    def _(i):
        wf[pl.ds(0, 1024), :] = praw[pl.ds(pl.multiple_of(i * 1024, 1024), 1024), :].astype(F32)
        at = pl.ds(pl.multiple_of(i * 512, 512), 512)
        pref[mine, 0, at, :] = wf[pl.ds(0, 512, stride=2), :].astype(BF)
        pref[mine, 1, at, :] = wf[pl.ds(1, 512, stride=2), :].astype(BF)

    pl.semaphore_wait(gate, len(peers))

    def item(dy, side, kv, part):
        hh = (1 - zh) if side else zh
        return rows(pref.at[((y + dy) % 4) * 4 + hh * 2 + core, kv], part)

    def put(name, dy, side, kv, part, key):
        r = item(dy, side, kv, part)
        m.send(name, r, r, p[key])

    def give(name, dx, zz, part, key):
        r = shard(dx, zz, part)
        m.send(name, r, r, p[key])

    def own(name, part, key):
        m.send(name, rows(hid, part), shard(0, zl, part), p[key])

    def fetch_w(half):
        first = pl.multiple_of((y * 2 + core) * WROWS + half * HALF, HALF)
        for d in (4, 2, 6, 1, 3, 5, 7):
            cols = pl.ds(pl.multiple_of((tp + d) % 8 * FEAT, FEAT), FEAT)
            m.send("w%d%d" % (half, d), wout.at[pl.ds(first, HALF), cols],
                   wcol.at[8 - d, pl.ds(first, HALF)], tp_peers[d - 1])

    def got_w(half):
        m.recv(*["w%d%d" % (half, d) for d in range(1, 8)])

    def piece_of(dy, half, size):
        first = pl.multiple_of((((y + dy) % 4) * 2 + core) * WROWS + half * HALF, HALF)
        return wcol.at[pl.ds(1, 7), pl.ds(first, size)]

    def pass_w(name, dy, half, key, size=HALF):
        ref = piece_of(dy, half, size)
        m.send(name, ref, ref, p[key])

    own("z1", H1, "zp")
    own("xp1", H1, "xp")
    own("xm2", H2, "xm")
    put("ypK", 0, 0, 0, PW, "yp")
    put("ymV", 0, 0, 1, PW, "ym")
    own("z2", H2, "zp")
    own("xp2", H2, "xp")
    own("xm1", H1, "xm")
    put("ypV", 0, 0, 1, PW, "yp")
    put("ymK", 0, 0, 0, PW, "ym")
    put("zKA", 0, 0, 0, PA, "zz")
    put("zVA", 0, 0, 1, PA, "zz")
    put("zKB", 0, 0, 0, PB, "zz")
    put("zVB", 0, 0, 1, PB, "zz")
    put("C0", 0, 0, 0, PW, "cc")
    put("C1", 0, 0, 1, PW, "cc")

    fetch_w(0)
    cp_h.wait()
    acc[...] = jnp.zeros_like(acc)
    sq[...] = jnp.zeros_like(sq)

    def compute(first, count, step, zz):
        @pl.loop(0, count)
        def _(j):
            s = ((x + first + step * j) % 4) * 2 + zz
            at = pl.multiple_of(s * FEAT, FEAT)
            wf[...] = wkv_v[pl.ds(pl.multiple_of(s * 2 * FEAT, 2 * FEAT), 2 * FEAT), :].astype(F32)
            wkvd[:, 0:HD] = wf[pl.ds(0, FEAT, stride=2), :].astype(BF)
            wkvd[:, HD:2 * HD] = wf[pl.ds(1, FEAT, stride=2), :].astype(BF)
            g = gain[s]

            @pl.loop(0, 2)
            def _(h):
                rr = pl.ds(pl.multiple_of(h * 256, 256), 256)
                xv = xbuf[s, rr, :].astype(F32)
                x2 = xv * xv
                t = x2[:, 0:128]
                for b in range(1, FEAT // 128):
                    t += x2[:, b * 128:(b + 1) * 128]
                sq[rr, :] += t
                xg = (xv * g).astype(BF)
                acc[rr, 0:512] += jnp.dot(xg, wq_v[pl.ds(at, FEAT), :], preferred_element_type=F32)
                acc[rr, 512:768] += jnp.dot(xg, wkvd[...], preferred_element_type=F32)

    cp_x.wait()
    cp_wq.wait()
    cp_wkv.wait()
    compute(0, 1, 1, zl)

    m.recv("xp1")
    give("fx1", 3, zl, H1, "xp")
    m.recv("xm2")
    give("fx2", 1, zl, H2, "xm")
    m.recv("ypK")
    put("fyK", 3, 0, 0, PW, "yp")
    put("zbK3", 3, 0, 0, PB, "zz")
    put("C2", 3, 0, 0, PW, "cc")
    m.recv("ymV")
    put("fyV", 1, 0, 1, PW, "ym")
    put("zbV1", 1, 0, 1, PB, "zz")
    put("C3", 1, 0, 1, PW, "cc")
    m.recv("z1")
    give("pxp1", 0, oz, H1, "xp")
    m.recv("z2")
    give("pxm2", 0, oz, H2, "xm")
    give("pxp2", 0, oz, H2, "xp")
    give("pxm1", 0, oz, H1, "xm")
    m.recv("xp2", "xm1")
    m.recv("ypV", "ymK")
    put("zbV3", 3, 0, 1, PB, "zz")
    put("zbK1", 1, 0, 0, PB, "zz")
    put("C4", 3, 0, 1, PW, "cc")
    put("C5", 1, 0, 0, PW, "cc")
    compute(3, 2, 2, zl)
    m.recv("zKA")
    put("zypK", 0, 1, 0, PA, "yp")
    put("zymK", 0, 1, 0, PA, "ym")
    put("C6", 0, 1, 0, PA, "cc")
    m.recv("fx1", "fx2")
    m.recv("fyK", "fyV")
    put("zbK2", 2, 0, 0, PB, "zz")
    put("zbV2", 2, 0, 1, PB, "zz")
    put("C7", 2, 0, 0, PW, "cc")
    put("C8", 2, 0, 1, PW, "cc")
    m.recv("zVA")
    put("zymV", 0, 1, 1, PA, "ym")
    put("zypV", 0, 1, 1, PA, "yp")
    put("C9", 0, 1, 1, PA, "cc")
    compute(2, 1, 1, zl)
    m.recv("pxp1")
    give("fpx1", 3, oz, H1, "xp")
    m.recv("pxm2")
    give("fpx2", 1, oz, H2, "xm")
    fetch_w(1)
    compute(0, 1, 1, oz)
    m.recv("zypK")
    put("fzK", 3, 1, 0, PA, "yp")
    put("C10", 3, 1, 0, PA, "cc")
    m.recv("zymV")
    put("fzV", 1, 1, 1, PA, "ym")
    put("C11", 1, 1, 1, PA, "cc")
    got_w(0)
    pass_w("wyp1", 0, 0, "yp")
    pass_w("wym1", 0, 0, "ym")
    m.recv("zKB", "zVB")
    put("C12", 0, 1, 0, PB, "cc")
    put("C13", 0, 1, 1, PB, "cc")
    m.recv("zbK3", "zbV1")
    put("C14", 3, 1, 0, PB, "cc")
    put("C15", 1, 1, 1, PB, "cc")
    m.recv("pxp2", "pxm1")
    compute(3, 2, 2, oz)
    m.recv("zbV3", "zbK1")
    put("C16", 3, 1, 1, PB, "cc")
    put("C17", 1, 1, 0, PB, "cc")
    m.recv("zypV", "zymK")
    put("C18", 3, 1, 1, PA, "cc")
    put("C19", 1, 1, 0, PA, "cc")
    m.recv("fpx1", "fpx2")
    compute(2, 1, 1, oz)
    c, s = cos[...], sin[...]

    def finish(r):
        rr = slice(r * 128, (r + 1) * 128)
        mean = jnp.sum(sq[rr, :], axis=-1, keepdims=True) * (1.0 / (8 * FEAT))
        scale = lax.rsqrt(mean + EPSILON)
        for g in range(4):
            v = acc[rr, g * HD:(g + 1) * HD] * scale
            q4[r, g * 128:(g + 1) * 128, :] = (v * c + pltpu.roll(v, HD // 2, 1) * s).astype(BF)
        v = acc[rr, 512:640] * scale
        k = v * c + pltpu.roll(v, HD // 2, 1) * s
        v = acc[rr, 640:768] * scale
        ks[r] = k.astype(BF)
        vs[r] = v.astype(BF)
        wf[pl.ds(0, 128, stride=2), :] = k
        wf[pl.ds(1, 128, stride=2), :] = v
        live = lax.broadcasted_iota(jnp.int32, (256, HD), 0) // 2 < lens[r]
        cache_v[r * 256:(r + 1) * 256, :] = jnp.where(live, wf[0:256, :], 0.0).astype(BF)

    finish(0)
    m.recv("zbK2", "zbV2")
    put("C20", 2, 1, 0, PB, "cc")
    put("C21", 2, 1, 1, PB, "cc")
    m.recv("fzK")
    put("C22", 2, 1, 0, PA, "cc")
    m.recv("fzV")
    put("C23", 2, 1, 1, PA, "cc")
    for i in range(24):
        m.recv("C%d" % i)

    factor = (HD ** -0.5) * 1.4426950408889634
    contract = (((1,), (1,)), ((), ()))

    def attend(r):
        slot = owners[groups[req * 4 + r]]
        length = lens[r]

        @pl.loop(0, 2)
        def _(i):
            q = q4[r, pl.ds(pl.multiple_of(i * 256, 256), 256), :]
            s1 = lax.dot_general(q, pref[slot, 0], contract, preferred_element_type=F32)
            s2 = lax.dot_general(q, ks[r], contract, preferred_element_type=F32)
            t = lax.broadcasted_iota(jnp.int32, (256, 128), 0) % 128
            pos = lax.broadcasted_iota(jnp.int32, (256, 128), 1)
            s2 = jnp.where((pos <= t) & (pos < length), s2, -jnp.inf)
            top = jnp.maximum(jnp.max(s1, axis=-1, keepdims=True), jnp.max(s2, axis=-1, keepdims=True))
            w1 = jnp.exp2((s1 - top) * factor)
            w2 = jnp.exp2((s2 - top) * factor)
            total = jnp.sum(w1, axis=-1, keepdims=True) + jnp.sum(w2, axis=-1, keepdims=True)
            o = jnp.dot(w1.astype(BF), pref[slot, 1], preferred_element_type=F32)
            o += jnp.dot(w2.astype(BF), vs[r], preferred_element_type=F32)
            o = (o / total).astype(BF)
            for j in range(2):
                lanes = pl.ds(pl.multiple_of((2 * i + j) * HD, HD), HD)
                ag[tp, r * 128:(r + 1) * 128, lanes] = o[j * 128:(j + 1) * 128, :]

    def rows_of(r):
        return (r * 128, 128), (r * 128, 64), (r * 128 + 64, 64)

    def pass_att(name, dx, zz, part, key):
        ref = rows(ag.at[((x + dx) % 4) * 2 + zz], part)
        m.send(name, ref, ref, p[key])

    def x_start(r, pre, zz):
        _, h1, h2 = rows_of(r)
        pass_att("%d%sxp1" % (r, pre), 0, zz, h1, "xp")
        pass_att("%d%sxm2" % (r, pre), 0, zz, h2, "xm")
        pass_att("%d%sxp2" % (r, pre), 0, zz, h2, "xp")
        pass_att("%d%sxm1" % (r, pre), 0, zz, h1, "xm")

    def x_forward(r, pre, zz):
        _, h1, h2 = rows_of(r)
        m.recv("%d%sxp1" % (r, pre))
        pass_att("%d%sfx1" % (r, pre), 3, zz, h1, "xp")
        m.recv("%d%sxm2" % (r, pre))
        pass_att("%d%sfx2" % (r, pre), 1, zz, h2, "xm")

    def x_near(r, pre):
        m.recv("%d%sxp2" % (r, pre), "%d%sxm1" % (r, pre))

    def x_far(r, pre):
        m.recv("%d%sfx1" % (r, pre), "%d%sfx2" % (r, pre))

    def z_pass(r, *shifts):
        for dx in shifts:
            pass_att("%dz%d" % (r, dx), dx, zl, rows_of(r)[0], "zp")

    def z_get(r, *shifts):
        m.recv(*["%dz%d" % (r, dx) for dx in shifts])

    def project(r, first, count, step, zz):
        @pl.loop(0, count)
        def _(j):
            t = ((x + first + step * j) % 4) * 2 + zz
            rr = slice(r * 128, r * 128 + 256)
            total[rr, :] += jnp.dot(ag[t, rr, :], wcol[(t - tp + 8) % 8], preferred_element_type=F32)

    def result(r):
        rr = slice(r * 128, (r + 1) * 128)
        live = lax.broadcasted_iota(jnp.int32, (128, FEAT), 0) < lens[r]
        out_v[rr, :] = jnp.where(live, hown[rr, :].astype(F32) + total[rr, :], 0.0).astype(BF)
        at = pl.ds(r * 128, 128)
        return local(out_v.at[at], out.at[at], 6 + r)

    attend(0)
    z_pass(0, 0)
    x_start(0, "", zl)
    total[...] = jnp.zeros_like(total)
    got_w(1)
    pass_w("wym2", 0, 1, "ym")
    pass_w("wyp2", 0, 1, "yp")
    pass_w("D0", 0, 0, "cc", WROWS)
    finish(1)
    attend(1)
    x_start(1, "", zl)
    z_pass(1, 0)
    x_forward(0, "", zl)
    z_get(0, 0)
    x_start(0, "p", oz)
    m.recv("wyp1")
    pass_w("wfx1", 3, 0, "yp")
    finish(2)
    attend(2)
    z_pass(2, 0)
    x_start(2, "", zl)
    x_forward(1, "", zl)
    x_near(1, "")
    z_pass(1, 1, 3)
    x_forward(0, "p", oz)
    finish(3)
    cp_c = local(cache_v, cache, 10)
    attend(3)
    x_start(3, "", zl)
    z_pass(3, 0)
    m.recv("wym2")
    pass_w("wfx2", 1, 1, "ym")
    x_far(1, "")
    z_pass(1, 2)
    x_forward(2, "", zl)
    z_get(2, 0)
    x_start(2, "p", oz)
    x_forward(3, "", zl)
    x_near(3, "")
    z_pass(3, 1, 3)
    m.recv("wyp2", "wym1")
    pass_w("D1", 3, 0, "cc", WROWS)
    pass_w("D2", 1, 0, "cc", WROWS)
    x_forward(2, "p", oz)
    m.recv("wfx1", "wfx2")
    pass_w("D3", 2, 0, "cc", WROWS)
    cp_w.wait()
    x_near(0, "")
    x_far(0, "")
    m.recv("D0", "D1", "D2", "D3")
    project(0, 0, 4, 1, zl)
    x_far(3, "")
    z_pass(3, 2)
    x_near(0, "p")
    x_far(0, "p")
    z_get(1, 0, 1, 2, 3)
    project(0, 0, 4, 1, oz)
    x_near(2, "")
    x_far(2, "")
    project(2, 0, 4, 1, zl)
    z_get(3, 0)
    project(2, 0, 1, 1, oz)
    leaving = [result(0), result(1)]
    x_near(2, "p")
    z_get(3, 1, 3)
    project(2, 3, 2, 2, oz)
    x_far(2, "p")
    z_get(3, 2)
    project(2, 2, 1, 1, oz)
    leaving += [result(2), result(3)]
    m.drain()
    cp_c.wait()
    for c in leaving:
        c.wait()
    assert len(m.made) == N_MAIL, len(m.made)


def emit_kernel(a, b, oa, ob, va, vb, sems):
    n = 4
    jobs = [(a, va, oa, i * (ROWS // n), ROWS // n) for i in range(n)] + [(b, vb, ob, 0, 2 * ROWS)]
    ins = []
    for i, (src, mid, _, first, size) in enumerate(jobs):
        at = pl.ds(first, size)
        c = pltpu.make_async_copy(src.at[at], mid.at[at], sems.at[i])
        c.start()
        ins.append(c)
    outs = []
    for i, (_, mid, dst, first, size) in enumerate(jobs):
        at = pl.ds(first, size)
        ins[i].wait()
        c = pltpu.make_async_copy(mid.at[at], dst.at[at], sems.at[len(jobs) + i])
        c.start()
        outs.append(c)
    for c in outs:
        c.wait()


def emit(a, b):
    hbm = pl.BlockSpec(memory_space=pl.ANY)
    return pl.pallas_call(
        emit_kernel,
        out_shape=(jax.ShapeDtypeStruct(a.shape, BF), jax.ShapeDtypeStruct(b.shape, BF)),
        in_specs=[hbm, hbm],
        out_specs=(hbm, hbm),
        scratch_shapes=[pltpu.VMEM(a.shape, BF), pltpu.VMEM(b.shape, BF), pltpu.SemaphoreType.DMA((10,))],
        name="emit",
    )(a, b)


def shards(hidden, norm_gain, w_query, w_kv, w_out, prefix_cache, lengths, groups, owners):
    n_req, suffix_len, feat = hidden.shape
    cos, sin = rope_tables()
    vm, hbm = pl.BlockSpec(memory_space=pltpu.VMEM), pl.BlockSpec(memory_space=pl.ANY)
    sm = pl.BlockSpec(memory_space=pltpu.SMEM)
    out, cache = pl.pallas_call(
        kernel,
        out_shape=(
            jax.ShapeDtypeStruct((ROWS, FEAT), BF),
            jax.ShapeDtypeStruct((2 * ROWS, HD), BF),
        ),
        in_specs=[sm, sm, sm, hbm, hbm, hbm, hbm, hbm, vm, vm, vm],
        out_specs=(hbm, hbm),
        scratch_shapes=[
            pltpu.VMEM((ROWS, FEAT), BF),
            pltpu.VMEM((2 * ROWS, HD), BF),
            pltpu.VMEM((8, ROWS, FEAT), BF),
            pltpu.VMEM((8 * FEAT, 512), BF),
            pltpu.VMEM((16 * FEAT, HD), BF),
            pltpu.VMEM((8, 512, FEAT), BF),
            pltpu.VMEM((2 * FEAT, HD), F32),
            pltpu.VMEM((FEAT, 2 * HD), BF),
            pltpu.VMEM((ROWS, FEAT), BF),
            pltpu.VMEM((2 * PREFIX, HD), BF),
            pltpu.VMEM((16, 2, PREFIX, HD), BF),
            pltpu.VMEM((ROWS, 768), F32),
            pltpu.VMEM((ROWS, HD), F32),
            pltpu.VMEM((4, 512, HD), BF),
            pltpu.VMEM((4, 128, HD), BF),
            pltpu.VMEM((4, 128, HD), BF),
            pltpu.VMEM((8, ROWS, 512), BF),
            pltpu.VMEM((ROWS, FEAT), F32),
            pltpu.SemaphoreType.DMA((N_MAIL,)),
            pltpu.SemaphoreType.DMA((N_MAIL,)),
            pltpu.SemaphoreType.DMA((11,)),
        ],
        compiler_params=pltpu.CompilerParams(
            collective_id=0, has_side_effects=True, vmem_limit_bytes=67043328),
        name="layer",
    )(
        lengths, groups, owners,
        hidden.reshape(ROWS, FEAT),
        prefix_cache.reshape(2 * PREFIX, HD),
        w_query,
        w_kv.reshape(16 * FEAT, HD),
        w_out,
        norm_gain.reshape(8, 1, FEAT),
        cos, sin)
    out, cache = emit(out, cache)
    return out.reshape(n_req, suffix_len, feat), cache.reshape(n_req, suffix_len, 2, HD)


def solution(mesh):
    return jax.shard_map(
        shards,
        mesh=mesh,
        in_specs=(
            P("req", None, "tp"),
            P(),
            P(None, "tp"),
            P(None, None, "tp"),
            P("tp", None),
            P("req", None, None, "tp"),
            P("req"),
            P(),
            P(),
        ),
        out_specs=(P("req", None, "tp"), P("req", None, None, "tp")),
        check_vma=False,
    )
```

```python
import jax
import jax.numpy as jnp
import numpy as np
from jax import lax
from jax.experimental import pallas as pl
from jax.experimental.pallas import tpu as pltpu
from jax.sharding import PartitionSpec as P

PREFIX = 2048
EPSILON = 1e-05
ROPE_BASE = 5000000.0
MESH = pl.DeviceIdType.MESH
BF = jnp.bfloat16
F32 = jnp.float32

ROWS = 512
FEAT = 896
HD = 128


PSPLIT = 1664
PA, PB, PW = (0, PSPLIT), (PSPLIT, PREFIX - PSPLIT), (0, PREFIX)
H1, H2 = (0, 256), (256, 256)
WROWS = 64
HALF = WROWS // 2
N_MAIL = 60 + 24 + 2 * 13 + 2 * 10


def rope_tables():
    f = np.float32
    positions = (PREFIX + np.arange(128)).astype(f)
    inverse = (f(ROPE_BASE) ** (-(f(2.0) * np.arange(HD // 2).astype(f)) / f(HD))).astype(f)
    angles = positions[:, None] * inverse[None, :]
    cosine = np.concatenate([np.cos(angles), np.cos(angles)], axis=-1)
    sine = np.concatenate([-np.sin(angles), np.sin(angles)], axis=-1)
    return cosine.astype(f), sine.astype(f)


def places():
    req, tp = lax.axis_index("req"), lax.axis_index("tp")
    x, zl = tp // 2, tp % 2
    y, low = req // 4, req % 4
    zh, core = low // 2, low % 2
    other_z = 1 - zl

    def at(xx, zz):
        return {"req": req, "tp": xx * 2 + zz}

    def own(yy, hh, cc):
        return {"req": yy * 4 + hh * 2 + cc, "tp": tp}

    return dict(
        req=req, tp=tp, x=x, zl=zl, y=y, zh=zh, core=core, oz=other_z,
        xp=at((x + 1) % 4, zl), xm=at((x + 3) % 4, zl), zp=at(x, other_z),
        yp=own((y + 1) % 4, zh, core), ym=own((y + 3) % 4, zh, core),
        zz=own(y, 1 - zh, core), cc=own(y, zh, 1 - core),
    )


class Mail:
    def __init__(self, send_sems, recv_sems):
        self.send_sems, self.recv_sems, self.made, self.left = send_sems, recv_sems, {}, []

    def send(self, name, src, dst, device):
        i = len(self.made)
        c = pltpu.make_async_remote_copy(
            src_ref=src, dst_ref=dst, send_sem=self.send_sems.at[i], recv_sem=self.recv_sems.at[i],
            device_id=device, device_id_type=MESH)
        c.start()
        self.made[name] = c
        self.left.append(c)

    def recv(self, *names):
        for name in names:
            self.made[name].wait_recv()

    def drain(self):
        for c in self.left:
            c.wait_send()
        self.left = []


def kernel(lens, groups, owners, hid, pre, wq, wkv, wout, gain, cos, sin, out, cache,
           out_v, cache_v, xbuf, wq_v, wkv_v, wcol, wf, wkvd, hown, praw, pref, acc, sq, q4, ks, vs, ag, total,
           send_sems, recv_sems, loc):
    p = places()
    req, tp, x, zl, oz = p["req"], p["tp"], p["x"], p["zl"], p["oz"]
    y, zh, core = p["y"], p["zh"], p["core"]
    tp_peers = [{"req": req, "tp": (tp + d) % 8} for d in range(1, 8)]
    peers = tp_peers + [p[k] for k in ("yp", "ym", "zz", "cc")]
    gate = pltpu.get_barrier_semaphore()
    for d in peers:
        pl.semaphore_signal(gate, inc=1, device_id=d, device_id_type=MESH)
    m = Mail(send_sems, recv_sems)

    def local(src, dst, i):
        c = pltpu.make_async_copy(src, dst, loc.at[i])
        c.start()
        return c

    def rows(ref, part):
        return ref.at[pl.ds(part[0], part[1])]

    def shard(dx, zz, part):
        return rows(xbuf.at[((x + dx) % 4) * 2 + zz], part)

    cp_pre = local(pre, praw, 0)
    cp_x = local(hid, xbuf.at[tp], 1)
    cp_wq = local(wq, wq_v, 2)
    cp_wkv = local(wkv, wkv_v, 3)
    cp_h = local(hid, hown, 4)
    cp_w = local(wout.at[:, pl.ds(pl.multiple_of(tp * FEAT, FEAT), FEAT)], wcol.at[0], 5)

    mine = y * 4 + zh * 2 + core
    cp_pre.wait()

    @pl.loop(0, 4)
    def _(i):
        wf[pl.ds(0, 1024), :] = praw[pl.ds(pl.multiple_of(i * 1024, 1024), 1024), :].astype(F32)
        at = pl.ds(pl.multiple_of(i * 512, 512), 512)
        pref[mine, 0, at, :] = wf[pl.ds(0, 512, stride=2), :].astype(BF)
        pref[mine, 1, at, :] = wf[pl.ds(1, 512, stride=2), :].astype(BF)

    pl.semaphore_wait(gate, len(peers))

    def item(dy, side, kv, part):
        hh = (1 - zh) if side else zh
        return rows(pref.at[((y + dy) % 4) * 4 + hh * 2 + core, kv], part)

    def put(name, dy, side, kv, part, key):
        r = item(dy, side, kv, part)
        m.send(name, r, r, p[key])

    def give(name, dx, zz, part, key):
        r = shard(dx, zz, part)
        m.send(name, r, r, p[key])

    def own(name, part, key):
        m.send(name, rows(hid, part), shard(0, zl, part), p[key])

    def fetch_w(half):
        first = pl.multiple_of((y * 2 + core) * WROWS + half * HALF, HALF)
        for d in (4, 2, 6, 1, 3, 5, 7):
            cols = pl.ds(pl.multiple_of((tp + d) % 8 * FEAT, FEAT), FEAT)
            m.send("w%d%d" % (half, d), wout.at[pl.ds(first, HALF), cols],
                   wcol.at[8 - d, pl.ds(first, HALF)], tp_peers[d - 1])

    def got_w(half):
        m.recv(*["w%d%d" % (half, d) for d in range(1, 8)])

    def piece_of(dy, half, size):
        first = pl.multiple_of((((y + dy) % 4) * 2 + core) * WROWS + half * HALF, HALF)
        return wcol.at[pl.ds(1, 7), pl.ds(first, size)]

    def pass_w(name, dy, half, key, size=HALF):
        ref = piece_of(dy, half, size)
        m.send(name, ref, ref, p[key])

    own("z1", H1, "zp")
    own("xp1", H1, "xp")
    own("xm2", H2, "xm")
    put("ypK", 0, 0, 0, PW, "yp")
    put("ymV", 0, 0, 1, PW, "ym")
    own("z2", H2, "zp")
    own("xp2", H2, "xp")
    own("xm1", H1, "xm")
    put("ypV", 0, 0, 1, PW, "yp")
    put("ymK", 0, 0, 0, PW, "ym")
    put("zKA", 0, 0, 0, PA, "zz")
    put("zVA", 0, 0, 1, PA, "zz")
    put("zKB", 0, 0, 0, PB, "zz")
    put("zVB", 0, 0, 1, PB, "zz")
    put("C0", 0, 0, 0, PW, "cc")
    put("C1", 0, 0, 1, PW, "cc")

    fetch_w(0)
    cp_h.wait()
    acc[...] = jnp.zeros_like(acc)
    sq[...] = jnp.zeros_like(sq)

    def compute(first, count, step, zz):
        @pl.loop(0, count)
        def _(j):
            s = ((x + first + step * j) % 4) * 2 + zz
            at = pl.multiple_of(s * FEAT, FEAT)
            wf[...] = wkv_v[pl.ds(pl.multiple_of(s * 2 * FEAT, 2 * FEAT), 2 * FEAT), :].astype(F32)
            wkvd[:, 0:HD] = wf[pl.ds(0, FEAT, stride=2), :].astype(BF)
            wkvd[:, HD:2 * HD] = wf[pl.ds(1, FEAT, stride=2), :].astype(BF)
            g = gain[s]

            @pl.loop(0, 2)
            def _(h):
                rr = pl.ds(pl.multiple_of(h * 256, 256), 256)
                xv = xbuf[s, rr, :].astype(F32)
                x2 = xv * xv
                t = x2[:, 0:128]
                for b in range(1, FEAT // 128):
                    t += x2[:, b * 128:(b + 1) * 128]
                sq[rr, :] += t
                xg = (xv * g).astype(BF)
                acc[rr, 0:512] += jnp.dot(xg, wq_v[pl.ds(at, FEAT), :], preferred_element_type=F32)
                acc[rr, 512:768] += jnp.dot(xg, wkvd[...], preferred_element_type=F32)

    cp_x.wait()
    cp_wq.wait()
    cp_wkv.wait()
    compute(0, 1, 1, zl)

    m.recv("xp1")
    give("fx1", 3, zl, H1, "xp")
    m.recv("xm2")
    give("fx2", 1, zl, H2, "xm")
    m.recv("ypK")
    put("fyK", 3, 0, 0, PW, "yp")
    put("zbK3", 3, 0, 0, PB, "zz")
    put("C2", 3, 0, 0, PW, "cc")
    m.recv("ymV")
    put("fyV", 1, 0, 1, PW, "ym")
    put("zbV1", 1, 0, 1, PB, "zz")
    put("C3", 1, 0, 1, PW, "cc")
    m.recv("z1")
    give("pxp1", 0, oz, H1, "xp")
    m.recv("z2")
    give("pxm2", 0, oz, H2, "xm")
    give("pxp2", 0, oz, H2, "xp")
    give("pxm1", 0, oz, H1, "xm")
    m.recv("xp2", "xm1")
    m.recv("ypV", "ymK")
    put("zbV3", 3, 0, 1, PB, "zz")
    put("zbK1", 1, 0, 0, PB, "zz")
    put("C4", 3, 0, 1, PW, "cc")
    put("C5", 1, 0, 0, PW, "cc")
    compute(3, 2, 2, zl)
    m.recv("zKA")
    put("zypK", 0, 1, 0, PA, "yp")
    put("zymK", 0, 1, 0, PA, "ym")
    put("C6", 0, 1, 0, PA, "cc")
    m.recv("fx1", "fx2")
    m.recv("fyK", "fyV")
    put("zbK2", 2, 0, 0, PB, "zz")
    put("zbV2", 2, 0, 1, PB, "zz")
    put("C7", 2, 0, 0, PW, "cc")
    put("C8", 2, 0, 1, PW, "cc")
    m.recv("zVA")
    put("zymV", 0, 1, 1, PA, "ym")
    put("zypV", 0, 1, 1, PA, "yp")
    put("C9", 0, 1, 1, PA, "cc")
    compute(2, 1, 1, zl)
    m.recv("pxp1")
    give("fpx1", 3, oz, H1, "xp")
    m.recv("pxm2")
    give("fpx2", 1, oz, H2, "xm")
    fetch_w(1)
    compute(0, 1, 1, oz)
    m.recv("zypK")
    put("fzK", 3, 1, 0, PA, "yp")
    put("C10", 3, 1, 0, PA, "cc")
    m.recv("zymV")
    put("fzV", 1, 1, 1, PA, "ym")
    put("C11", 1, 1, 1, PA, "cc")
    got_w(0)
    pass_w("wyp1", 0, 0, "yp")
    pass_w("wym1", 0, 0, "ym")
    m.recv("zKB", "zVB")
    put("C12", 0, 1, 0, PB, "cc")
    put("C13", 0, 1, 1, PB, "cc")
    m.recv("zbK3", "zbV1")
    put("C14", 3, 1, 0, PB, "cc")
    put("C15", 1, 1, 1, PB, "cc")
    m.recv("pxp2", "pxm1")
    compute(3, 2, 2, oz)
    m.recv("zbV3", "zbK1")
    put("C16", 3, 1, 1, PB, "cc")
    put("C17", 1, 1, 0, PB, "cc")
    m.recv("zypV", "zymK")
    put("C18", 3, 1, 1, PA, "cc")
    put("C19", 1, 1, 0, PA, "cc")
    m.recv("fpx1", "fpx2")
    compute(2, 1, 1, oz)
    c, s = cos[...], sin[...]

    def finish(r):
        rr = slice(r * 128, (r + 1) * 128)
        mean = jnp.sum(sq[rr, :], axis=-1, keepdims=True) * (1.0 / (8 * FEAT))
        scale = lax.rsqrt(mean + EPSILON)
        for g in range(4):
            v = acc[rr, g * HD:(g + 1) * HD] * scale
            q4[r, g * 128:(g + 1) * 128, :] = (v * c + pltpu.roll(v, HD // 2, 1) * s).astype(BF)
        v = acc[rr, 512:640] * scale
        k = v * c + pltpu.roll(v, HD // 2, 1) * s
        v = acc[rr, 640:768] * scale
        ks[r] = k.astype(BF)
        vs[r] = v.astype(BF)
        wf[pl.ds(0, 128, stride=2), :] = k
        wf[pl.ds(1, 128, stride=2), :] = v
        live = lax.broadcasted_iota(jnp.int32, (256, HD), 0) // 2 < lens[r]
        cache_v[r * 256:(r + 1) * 256, :] = jnp.where(live, wf[0:256, :], 0.0).astype(BF)

    finish(0)
    finish(1)
    m.recv("zbK2", "zbV2")
    put("C20", 2, 1, 0, PB, "cc")
    put("C21", 2, 1, 1, PB, "cc")
    m.recv("fzK")
    put("C22", 2, 1, 0, PA, "cc")
    m.recv("fzV")
    put("C23", 2, 1, 1, PA, "cc")
    for i in range(24):
        m.recv("C%d" % i)

    factor = (HD ** -0.5) * 1.4426950408889634
    contract = (((1,), (1,)), ((), ()))

    def attend(r):
        slot = owners[groups[req * 4 + r]]
        length = lens[r]

        @pl.loop(0, 2)
        def _(i):
            q = q4[r, pl.ds(pl.multiple_of(i * 256, 256), 256), :]
            s1 = lax.dot_general(q, pref[slot, 0], contract, preferred_element_type=F32)
            s2 = lax.dot_general(q, ks[r], contract, preferred_element_type=F32)
            t = lax.broadcasted_iota(jnp.int32, (256, 128), 0) % 128
            pos = lax.broadcasted_iota(jnp.int32, (256, 128), 1)
            s2 = jnp.where((pos <= t) & (pos < length), s2, -jnp.inf)
            top = jnp.maximum(jnp.max(s1, axis=-1, keepdims=True), jnp.max(s2, axis=-1, keepdims=True))
            w1 = jnp.exp2((s1 - top) * factor)
            w2 = jnp.exp2((s2 - top) * factor)
            total = jnp.sum(w1, axis=-1, keepdims=True) + jnp.sum(w2, axis=-1, keepdims=True)
            o = jnp.dot(w1.astype(BF), pref[slot, 1], preferred_element_type=F32)
            o += jnp.dot(w2.astype(BF), vs[r], preferred_element_type=F32)
            o = (o / total).astype(BF)
            for j in range(2):
                lanes = pl.ds(pl.multiple_of((2 * i + j) * HD, HD), HD)
                ag[tp, r * 128:(r + 1) * 128, lanes] = o[j * 128:(j + 1) * 128, :]

    def rows_of(r):
        return (r * 128, 128), (r * 128, 64), (r * 128 + 64, 64)

    def pass_att(name, dx, zz, part, key):
        ref = rows(ag.at[((x + dx) % 4) * 2 + zz], part)
        m.send(name, ref, ref, p[key])

    def x_start(r, pre, zz):
        _, h1, h2 = rows_of(r)
        pass_att("%d%sxp1" % (r, pre), 0, zz, h1, "xp")
        pass_att("%d%sxm2" % (r, pre), 0, zz, h2, "xm")
        pass_att("%d%sxp2" % (r, pre), 0, zz, h2, "xp")
        pass_att("%d%sxm1" % (r, pre), 0, zz, h1, "xm")

    def x_forward(r, pre, zz):
        _, h1, h2 = rows_of(r)
        m.recv("%d%sxp1" % (r, pre))
        pass_att("%d%sfx1" % (r, pre), 3, zz, h1, "xp")
        m.recv("%d%sxm2" % (r, pre))
        pass_att("%d%sfx2" % (r, pre), 1, zz, h2, "xm")

    def x_near(r, pre):
        m.recv("%d%sxp2" % (r, pre), "%d%sxm1" % (r, pre))

    def x_far(r, pre):
        m.recv("%d%sfx1" % (r, pre), "%d%sfx2" % (r, pre))

    def z_pass(r, *shifts):
        for dx in shifts:
            pass_att("%dz%d" % (r, dx), dx, zl, rows_of(r)[0], "zp")

    def z_get(r, *shifts):
        m.recv(*["%dz%d" % (r, dx) for dx in shifts])

    def project(r, first, count, step, zz):
        group = count

        @pl.loop(0, count // group)
        def _(j):
            rr = slice(r * 128, r * 128 + 256)
            add = None
            for i in range(group):
                t = ((x + first + step * (group * j + i)) % 4) * 2 + zz
                d = jnp.dot(ag[t, rr, :], wcol[(t - tp + 8) % 8], preferred_element_type=F32)
                add = d if add is None else add + d
            total[rr, :] += add

    def result(r):
        rr = slice(r * 128, (r + 1) * 128)
        live = lax.broadcasted_iota(jnp.int32, (128, FEAT), 0) < lens[r]
        out_v[rr, :] = jnp.where(live, hown[rr, :].astype(F32) + total[rr, :], 0.0).astype(BF)
        at = pl.ds(r * 128, 128)
        return local(out_v.at[at], out.at[at], 6 + r)

    attend(0)
    z_pass(0, 0)
    x_start(0, "", zl)
    total[...] = jnp.zeros_like(total)
    got_w(1)
    pass_w("wym2", 0, 1, "ym")
    pass_w("wyp2", 0, 1, "yp")
    pass_w("D0", 0, 0, "cc", WROWS)
    attend(1)
    x_start(1, "", zl)
    z_pass(1, 0)
    x_forward(0, "", zl)
    z_get(0, 0)
    x_start(0, "p", oz)
    m.recv("wyp1")
    pass_w("wfx1", 3, 0, "yp")
    finish(2)
    attend(2)
    z_pass(2, 0)
    x_start(2, "", zl)
    x_forward(1, "", zl)
    x_near(1, "")
    z_pass(1, 1, 3)
    x_forward(0, "p", oz)
    finish(3)
    cp_c = local(cache_v, cache, 10)
    attend(3)
    x_start(3, "", zl)
    z_pass(3, 0)
    m.recv("wym2")
    pass_w("wfx2", 1, 1, "ym")
    x_far(1, "")
    z_pass(1, 2)
    x_forward(2, "", zl)
    z_get(2, 0)
    x_start(2, "p", oz)
    x_forward(3, "", zl)
    x_near(3, "")
    z_pass(3, 1, 3)
    m.recv("wyp2", "wym1")
    pass_w("D1", 3, 0, "cc", WROWS)
    pass_w("D2", 1, 0, "cc", WROWS)
    x_forward(2, "p", oz)
    m.recv("wfx1", "wfx2")
    pass_w("D3", 2, 0, "cc", WROWS)
    cp_w.wait()
    x_near(0, "")
    x_far(0, "")
    m.recv("D0", "D1", "D2", "D3")
    project(0, 0, 4, 1, zl)
    x_far(3, "")
    z_pass(3, 2)
    x_near(0, "p")
    x_far(0, "p")
    z_get(1, 0, 1, 2, 3)
    project(0, 0, 4, 1, oz)
    x_near(2, "")
    x_far(2, "")
    project(2, 0, 4, 1, zl)
    z_get(3, 0)
    project(2, 0, 1, 1, oz)
    leaving = [result(0), result(1)]
    x_near(2, "p")
    z_get(3, 1, 3)
    project(2, 3, 2, 2, oz)
    x_far(2, "p")
    z_get(3, 2)
    project(2, 2, 1, 1, oz)
    leaving += [result(2), result(3)]
    m.drain()
    cp_c.wait()
    for c in leaving:
        c.wait()
    assert len(m.made) == N_MAIL, len(m.made)


def emit_kernel(a, b, oa, ob, va, vb, sems):
    n = 4
    jobs = [(a, va, oa, i * (ROWS // n), ROWS // n) for i in range(n)] + [(b, vb, ob, 0, 2 * ROWS)]
    ins = []
    for i, (src, mid, _, first, size) in enumerate(jobs):
        at = pl.ds(first, size)
        c = pltpu.make_async_copy(src.at[at], mid.at[at], sems.at[i])
        c.start()
        ins.append(c)
    outs = []
    for i, (_, mid, dst, first, size) in enumerate(jobs):
        at = pl.ds(first, size)
        ins[i].wait()
        c = pltpu.make_async_copy(mid.at[at], dst.at[at], sems.at[len(jobs) + i])
        c.start()
        outs.append(c)
    for c in outs:
        c.wait()


def emit(a, b):
    hbm = pl.BlockSpec(memory_space=pl.ANY)
    return pl.pallas_call(
        emit_kernel,
        out_shape=(jax.ShapeDtypeStruct(a.shape, BF), jax.ShapeDtypeStruct(b.shape, BF)),
        in_specs=[hbm, hbm],
        out_specs=(hbm, hbm),
        scratch_shapes=[pltpu.VMEM(a.shape, BF), pltpu.VMEM(b.shape, BF), pltpu.SemaphoreType.DMA((10,))],
        name="emit",
    )(a, b)


def shards(hidden, norm_gain, w_query, w_kv, w_out, prefix_cache, lengths, groups, owners):
    n_req, suffix_len, feat = hidden.shape
    cos, sin = rope_tables()
    vm, hbm = pl.BlockSpec(memory_space=pltpu.VMEM), pl.BlockSpec(memory_space=pl.ANY)
    sm = pl.BlockSpec(memory_space=pltpu.SMEM)
    out, cache = pl.pallas_call(
        kernel,
        out_shape=(
            jax.ShapeDtypeStruct((ROWS, FEAT), BF),
            jax.ShapeDtypeStruct((2 * ROWS, HD), BF),
        ),
        in_specs=[sm, sm, sm, hbm, hbm, hbm, hbm, hbm, vm, vm, vm],
        out_specs=(hbm, hbm),
        scratch_shapes=[
            pltpu.VMEM((ROWS, FEAT), BF),
            pltpu.VMEM((2 * ROWS, HD), BF),
            pltpu.VMEM((8, ROWS, FEAT), BF),
            pltpu.VMEM((8 * FEAT, 512), BF),
            pltpu.VMEM((16 * FEAT, HD), BF),
            pltpu.VMEM((8, 512, FEAT), BF),
            pltpu.VMEM((2 * FEAT, HD), F32),
            pltpu.VMEM((FEAT, 2 * HD), BF),
            pltpu.VMEM((ROWS, FEAT), BF),
            pltpu.VMEM((2 * PREFIX, HD), BF),
            pltpu.VMEM((16, 2, PREFIX, HD), BF),
            pltpu.VMEM((ROWS, 768), F32),
            pltpu.VMEM((ROWS, HD), F32),
            pltpu.VMEM((4, 512, HD), BF),
            pltpu.VMEM((4, 128, HD), BF),
            pltpu.VMEM((4, 128, HD), BF),
            pltpu.VMEM((8, ROWS, 512), BF),
            pltpu.VMEM((ROWS, FEAT), F32),
            pltpu.SemaphoreType.DMA((N_MAIL,)),
            pltpu.SemaphoreType.DMA((N_MAIL,)),
            pltpu.SemaphoreType.DMA((11,)),
        ],
        compiler_params=pltpu.CompilerParams(
            collective_id=0, has_side_effects=True, vmem_limit_bytes=67043328),
        name="layer",
    )(
        lengths, groups, owners,
        hidden.reshape(ROWS, FEAT),
        prefix_cache.reshape(2 * PREFIX, HD),
        w_query,
        w_kv.reshape(16 * FEAT, HD),
        w_out,
        norm_gain.reshape(8, 1, FEAT),
        cos, sin)
    out, cache = emit(out, cache)
    return out.reshape(n_req, suffix_len, feat), cache.reshape(n_req, suffix_len, 2, HD)


def solution(mesh):
    return jax.shard_map(
        shards,
        mesh=mesh,
        in_specs=(
            P("req", None, "tp"),
            P(),
            P(None, "tp"),
            P(None, None, "tp"),
            P("tp", None),
            P("req", None, None, "tp"),
            P("req"),
            P(),
            P(),
        ),
        out_specs=(P("req", None, "tp"), P("req", None, None, "tp")),
        check_vma=False,
    )
```
